512 devices in a mesh: space: 32 (over y_hi, z), design: 16 (over y_lo, x, core).
Axes of the slice: x: 4, y: 4 (y_hi: 2, y_lo: 2; y = y_hi * 2 + y_lo), z: 16, core: 2. Of those that a mesh axis runs over, the one named last changes fastest.
Arguments:
- states: float32 [16, 5, 128, 32, 128], P('design', None, 'space'), may hold values from -9 to 9
- source: float32 [5, 128, 32, 128], P(None, 'space'), may hold values from -6 to 6
- cell_kind: int32 [128, 32, 16], P('space'), may hold values from 0 to 2
- wall_points: int32 [15, 64], replicated, may hold values from 0 to 16383
- point_shape: float32 [15, 64, 5], replicated, may hold values from -8 to 8
- coupling: float32 [5, 5], replicated, may hold values from -0.45 to 0.45
Outputs:
- advanced: float32 [16, 5, 128, 32, 128], P('design', None, 'space')
The draws below stay inside these ranges and needn't reach their ends.
Inputs may be any that keep to these rules, and one draw needn't show every extreme that they name: `wall_points`: each value names the wall cell (x, 0, z) as x * 128 + z.
All inputs are finite; a program needn't handle non-finite values.
Results may differ from the reference program's by a relative error of at most 0.0003.
Values sent between devices are 32-bit elements; how exact they have to be, the bound alone decides.
A program may use at most 64 MiB of HBM per device.

```python
import jax
import jax.numpy as jnp
from jax import lax

FIELDS = 5
NY = 32
NZ = 128
ZB = 8
PTS = 64
SWEEPS = 4
PSTEPS = 2
MEMBERS = 16
TANGENTS = 15
NX = 128


def draw_states(key, part):
    keys = jax.random.split(jax.random.fold_in(key, 11), 3)
    grid = (NX, NY, NZ)
    large = 3.0 * jnp.clip(jax.random.normal(keys[0], (3,) + grid, jnp.float32), -3.0, 3.0)
    modest = jnp.clip(jax.random.normal(keys[1], (2,) + grid, jnp.float32), -4.0, 4.0)
    tangent_part = 2.0 * jnp.clip(jax.random.normal(keys[2], (MEMBERS - 1, FIELDS) + grid, jnp.float32), -4.0, 4.0)
    primal = jnp.stack([large[0], modest[0], large[1], large[2], 0.5 * large[0] + modest[1]])
    return jnp.concatenate([primal[None], tangent_part], axis=0).astype(jnp.float32)


def draw_coupling(key, part):
    keys = jax.random.split(jax.random.fold_in(key, 23), 2)
    magnitude = jax.random.uniform(keys[0], (FIELDS, FIELDS), jnp.float32, 0.25, 0.45)
    signs = jnp.where(jax.random.bernoulli(keys[1], 0.5, (FIELDS, FIELDS)), 1.0, -1.0)
    return (magnitude * signs).astype(jnp.float32)


def set_ends(drawn, own_key, low, largest):
    extent = drawn.shape
    spot = [jax.random.randint(jax.random.fold_in(own_key, axis), (), 0, extent[axis]) for axis in range(len(extent))]
    drawn = drawn.at[tuple(spot)].set(low)
    longest = extent.index(max(extent))
    spot[longest] = (spot[longest] + 1) % extent[longest]
    return drawn.at[tuple(spot)].set(largest)


def block_scale(key, shape, cuts, least, largest):
    def one(position, shards_of):
        heights = jax.random.uniform(jax.random.fold_in(jax.random.fold_in(key, 6), position), (shards_of,), jnp.float32, least / len(cuts), largest / len(cuts))
        return jnp.repeat(jnp.exp(heights), shape[position] // shards_of).reshape((-1,) + (1,) * (len(shape) - position - 1))

    gain = one(*cuts[0])
    for cut in cuts[1:]:
        gain = gain * one(*cut)
    return gain


def bell_draw(stream_key, extent, deviation, reach, pieces=(), held_as=jnp.bfloat16):
    entries = jax.random.normal(stream_key, extent, jnp.float32) * deviation
    if len(pieces) > 0:
        entries = block_scale(stream_key, extent, pieces, -0.22, 0.18) * entries
    return jnp.clip(entries, min=-reach, max=reach).astype(held_as)


def setup_inputs(seed: int = 0) -> dict:
    arg_keys = jax.random.split(jax.random.key(seed), 7)
    return {
        "states": draw_states(jax.random.fold_in(arg_keys[6], 71), 0),
        "source": bell_draw(arg_keys[1], (FIELDS, NX, NY, NZ), 1.0, 6.0, ((1, 32),), jnp.float32),
        "cell_kind": set_ends(jax.random.randint(arg_keys[2], (NX, NY, NZ // ZB), 0, 3), jax.random.fold_in(arg_keys[2], 1), 0, 2).astype(jnp.int32),
        "wall_points": set_ends(jax.random.randint(arg_keys[3], (TANGENTS, PTS), 0, NX * NZ), jax.random.fold_in(arg_keys[3], 1), 0, (NX * NZ) - 1).astype(jnp.int32),
        "point_shape": bell_draw(arg_keys[4], (TANGENTS, PTS, FIELDS), 2.0, 8.0, (), jnp.float32),
        "coupling": draw_coupling(jax.random.fold_in(arg_keys[6], 71), 0),
    }


def kind_term(cell_kind, block_cells):
    kind_cells = jnp.repeat(cell_kind, block_cells, axis=2)
    return 0.8 + 2.2 * (kind_cells == 1).astype(jnp.float32) + 0.7 * (kind_cells == 2).astype(jnp.float32)


def coefficient_fields(primal):
    blend = primal[4] - 0.5 * primal[0]
    return jnp.stack([jnp.exp(0.5 * jnp.tanh(blend)) - 1.0, jnp.tanh(primal[1])])


def wall_forcing(points, shapes, first_row, slab_rows, width_y, width_z):
    plane_cells = slab_rows * width_z
    local_index = points - first_row * width_z
    inside = (local_index >= 0) & (local_index < plane_cells)
    slot_index = jnp.where(inside, local_index, plane_cells).astype(jnp.int32)
    wall_plane = jnp.zeros((plane_cells, shapes.shape[1]), jnp.float32).at[slot_index].add(shapes.astype(jnp.float32), mode="drop")
    wall_plane = jnp.transpose(wall_plane).reshape(shapes.shape[1], slab_rows, 1, width_z)
    return jnp.pad(wall_plane, ((0, 0), (0, 0), (0, width_y - 1), (0, 0)))


def relax(unknowns, target, excess_nu, speed_excess, damping, coupling):
    padded = jnp.pad(unknowns, ((0, 0), (0, 0), (1, 1), (1, 1)))
    conduct = 1.0 + jnp.pad(excess_nu, ((0, 0), (1, 1), (1, 1)))
    centre_nu = conduct[1:-1, 1:-1, 1:-1]
    side_values = [conduct[:-2, 1:-1, 1:-1], conduct[2:, 1:-1, 1:-1], conduct[1:-1, :-2, 1:-1], conduct[1:-1, 2:, 1:-1], conduct[1:-1, 1:-1, :-2], conduct[1:-1, 1:-1, 2:]]
    neighbours = [padded[:, :-2, 1:-1, 1:-1], padded[:, 2:, 1:-1, 1:-1], padded[:, 1:-1, :-2, 1:-1], padded[:, 1:-1, 2:, 1:-1], padded[:, 1:-1, 1:-1, :-2], padded[:, 1:-1, 1:-1, 2:]]
    centre = padded[:, 1:-1, 1:-1, 1:-1]
    upwind = 1.0 + speed_excess
    diagonal = damping + upwind
    offdiag = upwind * neighbours[0]
    for side_nu, near_value in zip(side_values, neighbours):
        face_value = 0.5 * (centre_nu + side_nu)
        diagonal = diagonal + face_value
        offdiag = offdiag + face_value * near_value
    groups = centre.reshape((-1, coupling.shape[0]) + centre.shape[1:])
    coupled = jnp.einsum("fh,ghxyz->gfxyz", coupling, groups, precision=lax.Precision.HIGHEST).reshape(centre.shape)
    return centre + (target + offdiag - diagonal * centre - coupled) / diagonal


def pad_rows(values):
    widths = [(0, 0)] * values.ndim
    widths[-3] = (1, 1)
    return jnp.pad(values, widths)


def reference(states, source, cell_kind, wall_points, point_shape, coupling):
    damping = kind_term(cell_kind, ZB)
    members = jnp.arange(states.shape[0], dtype=jnp.int32)
    for pseudo_step in range(PSTEPS):
        coefficients = coefficient_fields(states[0])
        excess_nu = pad_rows(coefficients[0])
        speed_excess = coefficients[1]

        def advance(item):
            member, unknowns = item
            tangent_row = jnp.maximum(member - 1, 0).astype(jnp.int32)
            forcing = wall_forcing(wall_points[tangent_row], point_shape[tangent_row], 0, NX, NY, NZ)
            target = jnp.where(member == 0, source, forcing)
            for sweep_index in range(SWEEPS):
                unknowns = relax(pad_rows(unknowns), target, excess_nu, speed_excess, damping, coupling)
            return unknowns

        states = lax.map(advance, (members, states))
    return states
```

```python
import functools

import jax
import jax.numpy as jnp
from jax import lax
from jax.experimental import pallas as pl
from jax.experimental.pallas import tpu as pltpu
from jax.sharding import PartitionSpec as P

ZB = 8
SWEEPS = 4
PSTEPS = 2
FIELDS = 5
MESH = pl.DeviceIdType.MESH


def kernel(
    slabs, rows,
    u_ref, source_ref, kind_ref, points_ref, shapes_ref, coupling_ref,
    out_ref,
    ext, work, coef, weight, target, damping, kind_left, kind_right,
    u_send, u_recv, side_send, side_recv, coef_side, coef_send, coef_recv,
):
    space = lax.axis_index("space")
    design = lax.axis_index("design")
    width_y, width_z = u_ref.shape[2], u_ref.shape[3]
    wide = 3 * rows
    own = slice(rows, 2 * rows)
    lower = slice(0, rows)
    upper = slice(2 * rows, wide)
    parts = (own, lower, upper)

    core = design % 2
    ring = (design // 2) % 4
    pair = design // 8
    primal = design == 0
    has_left = space > 0
    has_right = space < slabs - 1
    relay = core == 0
    to_partner = relay
    to_pair = relay & (pair == 0)
    to_next = relay & (pair == 0) & (ring < 2)
    children = (
        (to_next, design + 2),
        (primal, design + 6),
        (to_pair, design + 8),
        (to_partner, design + 1),
    )
    last = ring // 3
    parent = core * (design - 1) + (1 - core) * (
        pair * (design - 8) + (1 - pair) * (1 - last) * (design - 2)
    )

    def remote(src, dst, send, recv, where):
        return pltpu.make_async_remote_copy(
            src_ref=src, dst_ref=dst, send_sem=send, recv_sem=recv, device_id=where, device_id_type=MESH
        )

    left = (space - 1, design)
    right = (space + 1, design)

    barrier = pltpu.get_barrier_semaphore()
    partners = [(has_left, left), (has_right, right), (design > 0, (space, parent))]
    partners += [(on, (space, child)) for on, child in children]
    expected = jnp.int32(0)
    for on, where in partners:
        expected = expected + on.astype(jnp.int32)

        @pl.when(on)
        def _(where=where):
            pl.semaphore_signal(barrier, inc=1, device_id=where, device_id_type=MESH)

    pl.semaphore_wait(barrier, expected)

    def u_copies(step):
        src = u_ref if step == 0 else ext.at[step, :, own]
        return (
            remote(src, ext.at[step, :, upper], u_send.at[step, 0], u_recv.at[step, 1], left),
            remote(src, ext.at[step, :, lower], u_send.at[step, 1], u_recv.at[step, 0], right),
        )

    kind_copies = (
        remote(kind_ref, kind_right, side_send.at[0], side_recv.at[1], left),
        remote(kind_ref, kind_left, side_send.at[1], side_recv.at[0], right),
    )
    source_copies = (
        remote(source_ref, target.at[:, upper], side_send.at[2], side_recv.at[3], left),
        remote(source_ref, target.at[:, lower], side_send.at[3], side_recv.at[2], right),
    )

    def coef_side_copies(step):
        src = coef.at[step, :, own]
        return (
            remote(src, coef.at[step, :, upper], coef_side.at[step, 0], coef_recv.at[step, 2], left),
            remote(src, coef.at[step, :, lower], coef_side.at[step, 1], coef_recv.at[step, 1], right),
        )

    def tree_copy(step, child, part):
        where = coef.at[step, :, parts[part]]
        return remote(where, where, coef_send.at[step, child, part], coef_recv.at[step, part], (space, children[child][1]))

    sides = (has_left, has_right)
    part_on = (None, has_left, has_right)

    def on_sides(copies, action, also=None):
        for on, copy in zip(sides, copies):

            @pl.when(on if also is None else on & also)
            def _(copy=copy):
                action(copy)

    def recv_sides(copies, also=None):
        for on, copy in zip(sides, copies[::-1]):

            @pl.when(on if also is None else on & also)
            def _(copy=copy):
                copy.wait_recv()

    def start(copy):
        copy.start()

    def wait_send(copy):
        copy.wait_send()

    def forward(step, part, action):
        for child, (on, _) in enumerate(children):
            here = on if part_on[part] is None else on & part_on[part]

            @pl.when(here)
            def _(child=child):
                action(tree_copy(step, child, part))

    def primal_coefficients(step):
        @pl.when(primal)
        def _():
            def row(r, carry):
                if step == 0:
                    p0, p1, p4 = u_ref[0, r], u_ref[1, r], u_ref[4, r]
                else:
                    p0, p1, p4 = ext[step, 0, rows + r], ext[step, 1, rows + r], ext[step, 4, rows + r]
                coef[step, 0, rows + r] = jnp.exp(0.5 * jnp.tanh(p4 - 0.5 * p0)) - 1.0
                coef[step, 1, rows + r] = jnp.tanh(p1)
                return carry

            lax.fori_loop(0, rows, row, 0)

    def blank(step):
        @pl.when(space == 0)
        def _():
            ext[step, :, lower] = jnp.zeros((FIELDS, rows, width_y, width_z), jnp.float32)
            coef[step, :, lower] = jnp.zeros((2, rows, width_y, width_z), jnp.float32)

        @pl.when(space == slabs - 1)
        def _():
            ext[step, :, upper] = jnp.zeros((FIELDS, rows, width_y, width_z), jnp.float32)
            coef[step, :, upper] = jnp.zeros((2, rows, width_y, width_z), jnp.float32)

    row_y = lax.broadcasted_iota(jnp.int32, (width_y, width_z), 0)
    row_z = lax.broadcasted_iota(jnp.int32, (width_y, width_z), 1)
    first_y, last_y = row_y == 0, row_y == width_y - 1
    first_z, last_z = row_z == 0, row_z == width_z - 1

    def shifts(plane):
        return (
            pltpu.roll(plane, 1, 0),
            pltpu.roll(plane, width_y - 1, 0),
            pltpu.roll(plane, 1, 1),
            pltpu.roll(plane, width_z - 1, 1),
        )

    edges = (first_y, last_y, first_z, last_z)

    def weights(step):
        def row(r, carry):
            centre = 1.0 + coef[step, 0, r]
            below = 0.5 * (centre + 1.0 + coef[step, 0, r - 1])
            above = 0.5 * (centre + 1.0 + coef[step, 0, r + 1])
            upwind = 1.0 + coef[step, 1, r]
            diagonal = damping[r] + upwind + below + above
            grid_row = space * rows + r - rows
            weight[0, r] = jnp.where(grid_row == 0, 0.0, below + upwind)
            weight[1, r] = jnp.where(grid_row == slabs * rows - 1, 0.0, above)
            for k, (near, edge) in enumerate(zip(shifts(centre), edges)):
                face = 0.5 * (centre + jnp.where(edge, 1.0, near))
                diagonal = diagonal + face
                weight[2 + k, r] = jnp.where(edge, 0.0, face)
            weight[6, r] = 1.0 / diagonal
            return carry

        lax.fori_loop(1, wide - 1, row, 0)

    def sweep(src, dst, lo, hi, shift):
        def row(r, carry):
            planes = [src[f, r] for f in range(FIELDS)]
            for f in range(FIELDS):
                total = target[f, r] + weight[0, r] * src[f, r - 1] + weight[1, r] * src[f, r + 1]
                for k, near in enumerate(shifts(planes[f])):
                    total = total + weight[2 + k, r] * near
                for h in range(FIELDS):
                    total = total - coupling_ref[f, h] * planes[h]
                dst[f, r - shift] = total * weight[6, r]
            return carry

        lax.fori_loop(lo, hi, row, 0)

    def spread_kinds(kinds, first):
        blocks = kinds[...].astype(jnp.float32).reshape(rows * width_y, width_z // ZB)
        pick_b = lax.broadcasted_iota(jnp.int32, (width_z // ZB, width_z), 0)
        pick_z = lax.broadcasted_iota(jnp.int32, (width_z // ZB, width_z), 1)
        inside = (pick_z >= pick_b * ZB) & (pick_z < pick_b * ZB + ZB)
        cells = jnp.dot(blocks, inside.astype(jnp.float32), preferred_element_type=jnp.float32)
        value = 0.8 + jnp.where(cells == 1.0, 2.2, 0.0) + jnp.where(cells == 2.0, 0.7, 0.0)
        damping[first : first + rows] = value.reshape(rows, width_y, width_z)

    on_sides(kind_copies, start)
    primal_coefficients(0)
    on_sides(coef_side_copies(0), start, primal)

    @pl.when(primal)
    def _():
        forward(0, 0, start)

    on_sides(u_copies(0), start)
    on_sides(source_copies, start, primal)

    blank(0)
    ext[0, :, own] = u_ref[...]

    @pl.when(primal)
    def _():
        target[:, own] = source_ref[...]

        @pl.when(space == 0)
        def _():
            target[:, lower] = jnp.zeros((FIELDS, rows, width_y, width_z), jnp.float32)

        @pl.when(space == slabs - 1)
        def _():
            target[:, upper] = jnp.zeros((FIELDS, rows, width_y, width_z), jnp.float32)

    @pl.when(design > 0)
    def _():
        def row(r, carry):
            cell = (space * rows + r - rows) * width_z + lax.broadcasted_iota(
                jnp.int32, (width_z, points_ref.shape[1]), 0
            )
            hit = (points_ref[...] == cell).astype(jnp.float32)
            wall = lax.dot_general(
                shapes_ref[...], hit, (((1,), (1,)), ((), ())),
                precision=lax.Precision.HIGHEST, preferred_element_type=jnp.float32,
            )
            for f in range(FIELDS):
                line = jnp.broadcast_to(wall[f : f + 1], (width_y, width_z))
                target[f, r] = jnp.where(first_y, line, 0.0)
            return carry

        lax.fori_loop(0, wide, row, 0)

    spread_kinds(kind_ref, rows)

    for step in range(PSTEPS):
        if step > 0:
            primal_coefficients(step)
            on_sides(coef_side_copies(step), start, primal)

            @pl.when(primal)
            def _():
                forward(step, 0, start)

            on_sides(u_copies(step), start)
            blank(step)

        for part in range(3):
            waits = design > 0 if part == 0 else part_on[part]

            @pl.when(waits)
            def _():
                tree_copy(step, 0, part).wait_recv()

            if part == 0:

                @pl.when(design > 0)
                def _():
                    forward(step, part, start)

            else:
                forward(step, part, start)

        if step == 0:
            recv_sides(kind_copies)

            @pl.when(has_left)
            def _():
                spread_kinds(kind_left, 0)

            @pl.when(has_right)
            def _():
                spread_kinds(kind_right, 2 * rows)

            @pl.when(space == 0)
            def _():
                damping[lower] = jnp.zeros((rows, width_y, width_z), jnp.float32)

            @pl.when(space == slabs - 1)
            def _():
                damping[upper] = jnp.zeros((rows, width_y, width_z), jnp.float32)

        weights(step)
        if step == 0:
            recv_sides(source_copies, primal)
        recv_sides(u_copies(step))

        now = ext.at[step]
        for sweep_index in range(SWEEPS):
            margin = sweep_index + 1
            if sweep_index < SWEEPS - 1:
                later = work.at[sweep_index % 2]
                sweep(now, later, margin, wide - margin, 0)
                now = later
            elif step < PSTEPS - 1:
                sweep(now, ext.at[step + 1], margin, wide - margin, 0)
            else:
                sweep(now, out_ref, margin, wide - margin, rows)

    on_sides(kind_copies, wait_send)
    on_sides(source_copies, wait_send, primal)
    for step in range(PSTEPS):
        on_sides(u_copies(step), wait_send)
        on_sides(coef_side_copies(step), wait_send, primal)
        for part in range(3):
            forward(step, part, wait_send)


def shards(states, source, cell_kind, wall_points, point_shape, coupling):
    member_state = states[0]
    fields, rows, width_y, width_z = member_state.shape
    slabs = lax.axis_size("space")
    tangent_row = jnp.maximum(lax.axis_index("design") - 1, 0)
    points = lax.dynamic_slice_in_dim(wall_points, tangent_row, 1, 0)
    shapes = jnp.transpose(lax.dynamic_index_in_dim(point_shape, tangent_row, 0, keepdims=False))
    shapes = jnp.pad(shapes, ((0, 8 - fields), (0, 0)))
    vmem = pl.BlockSpec(memory_space=pltpu.VMEM)
    wide = 3 * rows
    out = pl.pallas_call(
        functools.partial(kernel, slabs, rows),
        name="sweeps",
        out_shape=jax.ShapeDtypeStruct(member_state.shape, jnp.float32),
        in_specs=[vmem] * 5 + [pl.BlockSpec(memory_space=pltpu.SMEM)],
        out_specs=vmem,
        scratch_shapes=[
            pltpu.VMEM((PSTEPS, fields, wide, width_y, width_z), jnp.float32),
            pltpu.VMEM((2, fields, wide, width_y, width_z), jnp.float32),
            pltpu.VMEM((PSTEPS, 2, wide, width_y, width_z), jnp.float32),
            pltpu.VMEM((7, wide, width_y, width_z), jnp.float32),
            pltpu.VMEM((fields, wide, width_y, width_z), jnp.float32),
            pltpu.VMEM((wide, width_y, width_z), jnp.float32),
            pltpu.VMEM(cell_kind.shape, jnp.int32),
            pltpu.VMEM(cell_kind.shape, jnp.int32),
            pltpu.SemaphoreType.DMA((PSTEPS, 2)),
            pltpu.SemaphoreType.DMA((PSTEPS, 2)),
            pltpu.SemaphoreType.DMA((4,)),
            pltpu.SemaphoreType.DMA((4,)),
            pltpu.SemaphoreType.DMA((PSTEPS, 2)),
            pltpu.SemaphoreType.DMA((PSTEPS, 4, 3)),
            pltpu.SemaphoreType.DMA((PSTEPS, 3)),
        ],
        compiler_params=pltpu.CompilerParams(collective_id=0, has_side_effects=True),
    )(member_state, source, cell_kind, points, shapes, coupling)
    return out[None]


def solution(mesh):
    in_specs = (
        P("design", None, "space", None, None),
        P(None, "space", None, None),
        P("space", None, None),
        P(),
        P(),
        P(),
    )
    out_specs = P("design", None, "space", None, None)
    return jax.shard_map(shards, mesh=mesh, in_specs=in_specs, out_specs=out_specs, check_vma=False)
```

```python
import functools

import jax
import jax.numpy as jnp
from jax import lax
from jax.experimental import pallas as pl
from jax.experimental.pallas import tpu as pltpu
from jax.sharding import PartitionSpec as P

ZB = 8
SWEEPS = 4
PSTEPS = 2
FIELDS = 5
MESH = pl.DeviceIdType.MESH


def kernel(
    slabs, rows,
    u_ref, source_ref, kind_ref, points_ref, shapes_ref, coupling_ref,
    out_ref,
    ext, work, coef, weight, target, damping, kind_left, kind_right,
    u_send, u_recv, side_send, side_recv, coef_side, coef_send, coef_recv,
):
    space = lax.axis_index("space")
    design = lax.axis_index("design")
    width_y, width_z = u_ref.shape[2], u_ref.shape[3]
    wide = 3 * rows
    own = slice(rows, 2 * rows)
    lower = slice(0, rows)
    upper = slice(2 * rows, wide)
    parts = (own, lower, upper)

    core = design % 2
    ring = (design // 2) % 4
    pair = design // 8
    primal = design == 0
    has_left = space > 0
    has_right = space < slabs - 1
    relay = core == 0
    to_partner = relay
    to_pair = relay & (pair == 0)
    to_next = relay & (pair == 0) & (ring < 2)
    children = (
        (to_next, design + 2),
        (primal, design + 6),
        (to_pair, design + 8),
        (to_partner, design + 1),
    )
    last = ring // 3
    parent = core * (design - 1) + (1 - core) * (
        pair * (design - 8) + (1 - pair) * (1 - last) * (design - 2)
    )

    def remote(src, dst, send, recv, where):
        return pltpu.make_async_remote_copy(
            src_ref=src, dst_ref=dst, send_sem=send, recv_sem=recv, device_id=where, device_id_type=MESH
        )

    left = (space - 1, design)
    right = (space + 1, design)

    barrier = pltpu.get_barrier_semaphore()
    partners = [(has_left, left), (has_right, right), (design > 0, (space, parent))]
    partners += [(on, (space, child)) for on, child in children]
    expected = jnp.int32(0)
    for on, where in partners:
        expected = expected + on.astype(jnp.int32)

        @pl.when(on)
        def _(where=where):
            pl.semaphore_signal(barrier, inc=1, device_id=where, device_id_type=MESH)

    pl.semaphore_wait(barrier, expected)

    def u_copies(step):
        src = u_ref if step == 0 else ext.at[step, :, own]
        return (
            remote(src, ext.at[step, :, upper], u_send.at[step, 0], u_recv.at[step, 1], left),
            remote(src, ext.at[step, :, lower], u_send.at[step, 1], u_recv.at[step, 0], right),
        )

    kind_copies = (
        remote(kind_ref, kind_right, side_send.at[0], side_recv.at[1], left),
        remote(kind_ref, kind_left, side_send.at[1], side_recv.at[0], right),
    )
    source_copies = (
        remote(source_ref, target.at[:, upper], side_send.at[2], side_recv.at[3], left),
        remote(source_ref, target.at[:, lower], side_send.at[3], side_recv.at[2], right),
    )

    def coef_side_copies(step):
        src = coef.at[step, :, own]
        return (
            remote(src, coef.at[step, :, upper], coef_side.at[step, 0], coef_recv.at[step, 2], left),
            remote(src, coef.at[step, :, lower], coef_side.at[step, 1], coef_recv.at[step, 1], right),
        )

    def tree_copy(step, child, part):
        where = coef.at[step, :, parts[part]]
        return remote(where, where, coef_send.at[step, child, part], coef_recv.at[step, part], (space, children[child][1]))

    sides = (has_left, has_right)
    part_on = (None, has_left, has_right)

    def on_sides(copies, action, also=None):
        for on, copy in zip(sides, copies):

            @pl.when(on if also is None else on & also)
            def _(copy=copy):
                action(copy)

    def recv_sides(copies, also=None):
        for on, copy in zip(sides, copies[::-1]):

            @pl.when(on if also is None else on & also)
            def _(copy=copy):
                copy.wait_recv()

    def start(copy):
        copy.start()

    def wait_send(copy):
        copy.wait_send()

    def forward(step, part, action):
        for child, (on, _) in enumerate(children):
            here = on if part_on[part] is None else on & part_on[part]

            @pl.when(here)
            def _(child=child):
                action(tree_copy(step, child, part))

    def primal_coefficients(step):
        @pl.when(primal)
        def _():
            def row(r, carry):
                if step == 0:
                    p0, p1, p4 = u_ref[0, r], u_ref[1, r], u_ref[4, r]
                else:
                    p0, p1, p4 = ext[step, 0, rows + r], ext[step, 1, rows + r], ext[step, 4, rows + r]
                coef[step, 0, rows + r] = jnp.exp(0.5 * jnp.tanh(p4 - 0.5 * p0)) - 1.0
                coef[step, 1, rows + r] = jnp.tanh(p1)
                return carry

            lax.fori_loop(0, rows, row, 0)

    def blank(step):
        @pl.when(space == 0)
        def _():
            ext[step, :, lower] = jnp.zeros((FIELDS, rows, width_y, width_z), jnp.float32)
            coef[step, :, lower] = jnp.zeros((2, rows, width_y, width_z), jnp.float32)

        @pl.when(space == slabs - 1)
        def _():
            ext[step, :, upper] = jnp.zeros((FIELDS, rows, width_y, width_z), jnp.float32)
            coef[step, :, upper] = jnp.zeros((2, rows, width_y, width_z), jnp.float32)

    row_y = lax.broadcasted_iota(jnp.int32, (width_y, width_z), 0)
    row_z = lax.broadcasted_iota(jnp.int32, (width_y, width_z), 1)
    first_y, last_y = row_y == 0, row_y == width_y - 1
    first_z, last_z = row_z == 0, row_z == width_z - 1

    def shifts(plane):
        return (
            pltpu.roll(plane, 1, 0),
            pltpu.roll(plane, width_y - 1, 0),
            pltpu.roll(plane, 1, 1),
            pltpu.roll(plane, width_z - 1, 1),
        )

    edges = (first_y, last_y, first_z, last_z)

    def weights(step):
        def row(r, carry):
            centre = 1.0 + coef[step, 0, r]
            below = 0.5 * (centre + 1.0 + coef[step, 0, r - 1])
            above = 0.5 * (centre + 1.0 + coef[step, 0, r + 1])
            upwind = 1.0 + coef[step, 1, r]
            diagonal = damping[r] + upwind + below + above
            grid_row = space * rows + r - rows
            weight[0, r] = jnp.where(grid_row == 0, 0.0, below + upwind)
            weight[1, r] = jnp.where(grid_row == slabs * rows - 1, 0.0, above)
            for k, (near, edge) in enumerate(zip(shifts(centre), edges)):
                face = 0.5 * (centre + jnp.where(edge, 1.0, near))
                diagonal = diagonal + face
                weight[2 + k, r] = jnp.where(edge, 0.0, face)
            weight[6, r] = 1.0 / diagonal
            return carry

        lax.fori_loop(1, wide - 1, row, 0)

    def sweep(src, dst, lo, hi, shift):
        def row(r, carry):
            planes = [src[f, r] for f in range(FIELDS)]
            for f in range(FIELDS):
                total = target[f, r] + weight[0, r] * src[f, r - 1] + weight[1, r] * src[f, r + 1]
                for k, near in enumerate(shifts(planes[f])):
                    total = total + weight[2 + k, r] * near
                for h in range(FIELDS):
                    total = total - coupling_ref[f, h] * planes[h]
                dst[f, r - shift] = total * weight[6, r]
            return carry

        lax.fori_loop(lo, hi, row, 0)

    def spread_kinds(kinds, first):
        pick_b = lax.broadcasted_iota(jnp.int32, (width_z // ZB, width_z), 0)
        pick_z = lax.broadcasted_iota(jnp.int32, (width_z // ZB, width_z), 1)
        inside = (pick_z >= pick_b * ZB) & (pick_z < pick_b * ZB + ZB)
        for r in range(rows):
            cells = lax.dot_general(
                kinds[r].astype(jnp.float32), inside.astype(jnp.float32), (((0,), (0,)), ((), ())),
                preferred_element_type=jnp.float32,
            )
            damping[first + r] = 0.8 + jnp.where(cells == 1.0, 2.2, 0.0) + jnp.where(cells == 2.0, 0.7, 0.0)

    on_sides(kind_copies, start)
    primal_coefficients(0)
    on_sides(coef_side_copies(0), start, primal)

    @pl.when(primal)
    def _():
        forward(0, 0, start)

    on_sides(u_copies(0), start)
    on_sides(source_copies, start, primal)

    blank(0)
    ext[0, :, own] = u_ref[...]

    @pl.when(primal)
    def _():
        target[:, own] = source_ref[...]

        @pl.when(space == 0)
        def _():
            target[:, lower] = jnp.zeros((FIELDS, rows, width_y, width_z), jnp.float32)

        @pl.when(space == slabs - 1)
        def _():
            target[:, upper] = jnp.zeros((FIELDS, rows, width_y, width_z), jnp.float32)

    @pl.when(design > 0)
    def _():
        tangents, count = points_ref.shape
        mine = lax.broadcasted_iota(jnp.int32, (tangents, count), 0) == design - 1
        points = jnp.sum(jnp.where(mine, points_ref[...], 0), axis=0, keepdims=True)
        shapes = jnp.concatenate(
            [
                jnp.sum(jnp.where(mine, shapes_ref[f], 0.0), axis=0, keepdims=True)
                for f in range(FIELDS)
            ],
            axis=0,
        )

        def row(r, carry):
            cell = (space * rows + r - rows) * width_z + lax.broadcasted_iota(
                jnp.int32, (width_z, count), 0
            )
            hit = (points == cell).astype(jnp.float32)
            wall = lax.dot_general(
                shapes, hit, (((1,), (1,)), ((), ())),
                precision=lax.Precision.HIGHEST, preferred_element_type=jnp.float32,
            )
            for f in range(FIELDS):
                line = jnp.broadcast_to(wall[f : f + 1], (width_y, width_z))
                target[f, r] = jnp.where(first_y, line, 0.0)
            return carry

        lax.fori_loop(0, wide, row, 0)

    spread_kinds(kind_ref, rows)

    for step in range(PSTEPS):
        if step > 0:
            primal_coefficients(step)
            on_sides(coef_side_copies(step), start, primal)

            @pl.when(primal)
            def _():
                forward(step, 0, start)

            on_sides(u_copies(step), start)
            blank(step)

        for part in range(3):
            waits = design > 0 if part == 0 else part_on[part]

            @pl.when(waits)
            def _():
                tree_copy(step, 0, part).wait_recv()

            if part == 0:

                @pl.when(design > 0)
                def _():
                    forward(step, part, start)

            else:
                forward(step, part, start)

        if step == 0:
            recv_sides(kind_copies)

            @pl.when(has_left)
            def _():
                spread_kinds(kind_left, 0)

            @pl.when(has_right)
            def _():
                spread_kinds(kind_right, 2 * rows)

            @pl.when(space == 0)
            def _():
                damping[lower] = jnp.zeros((rows, width_y, width_z), jnp.float32)

            @pl.when(space == slabs - 1)
            def _():
                damping[upper] = jnp.zeros((rows, width_y, width_z), jnp.float32)

        weights(step)
        if step == 0:
            recv_sides(source_copies, primal)
        recv_sides(u_copies(step))

        now = ext.at[step]
        for sweep_index in range(SWEEPS):
            margin = sweep_index + 1
            if sweep_index < SWEEPS - 1:
                later = work.at[sweep_index % 2]
                sweep(now, later, margin, wide - margin, 0)
                now = later
            elif step < PSTEPS - 1:
                sweep(now, ext.at[step + 1], margin, wide - margin, 0)
            else:
                sweep(now, out_ref, margin, wide - margin, rows)

    on_sides(kind_copies, wait_send)
    on_sides(source_copies, wait_send, primal)
    for step in range(PSTEPS):
        on_sides(u_copies(step), wait_send)
        on_sides(coef_side_copies(step), wait_send, primal)
        for part in range(3):
            forward(step, part, wait_send)


def shards(states, source, cell_kind, wall_points, point_shape, coupling):
    member_state = states[0]
    fields, rows, width_y, width_z = member_state.shape
    slabs = lax.axis_size("space")
    kinds = jnp.transpose(cell_kind, (0, 2, 1))
    shapes = jnp.transpose(point_shape, (2, 0, 1))
    vmem = pl.BlockSpec(memory_space=pltpu.VMEM)
    wide = 3 * rows
    out = pl.pallas_call(
        functools.partial(kernel, slabs, rows),
        name="sweeps",
        out_shape=pltpu.VMEM(member_state.shape, jnp.float32),
        in_specs=[vmem] * 5 + [pl.BlockSpec(memory_space=pltpu.SMEM)],
        out_specs=vmem,
        scratch_shapes=[
            pltpu.VMEM((PSTEPS, fields, wide, width_y, width_z), jnp.float32),
            pltpu.VMEM((2, fields, wide, width_y, width_z), jnp.float32),
            pltpu.VMEM((PSTEPS, 2, wide, width_y, width_z), jnp.float32),
            pltpu.VMEM((7, wide, width_y, width_z), jnp.float32),
            pltpu.VMEM((fields, wide, width_y, width_z), jnp.float32),
            pltpu.VMEM((wide, width_y, width_z), jnp.float32),
            pltpu.VMEM(kinds.shape, jnp.int32),
            pltpu.VMEM(kinds.shape, jnp.int32),
            pltpu.SemaphoreType.DMA((PSTEPS, 2)),
            pltpu.SemaphoreType.DMA((PSTEPS, 2)),
            pltpu.SemaphoreType.DMA((4,)),
            pltpu.SemaphoreType.DMA((4,)),
            pltpu.SemaphoreType.DMA((PSTEPS, 2)),
            pltpu.SemaphoreType.DMA((PSTEPS, 4, 3)),
            pltpu.SemaphoreType.DMA((PSTEPS, 3)),
        ],
        compiler_params=pltpu.CompilerParams(collective_id=0, has_side_effects=True),
    )(member_state, source, kinds, wall_points, shapes, coupling)
    return out[None]


def solution(mesh):
    in_specs = (
        P("design", None, "space", None, None),
        P(None, "space", None, None),
        P("space", None, None),
        P(),
        P(),
        P(),
    )
    out_specs = P("design", None, "space", None, None)
    return jax.shard_map(shards, mesh=mesh, in_specs=in_specs, out_specs=out_specs, check_vma=False)
```

```python
import functools

import jax
import jax.numpy as jnp
from jax import lax
from jax.experimental import pallas as pl
from jax.experimental.pallas import tpu as pltpu
from jax.sharding import PartitionSpec as P

ZB = 8
SWEEPS = 4
PSTEPS = 2
FIELDS = 5
MESH = pl.DeviceIdType.MESH


def kernel(
    slabs, rows,
    u_ref, source_ref, kind_ref, points_ref, shapes_ref, coupling_ref,
    out_ref,
    level, coef, weight, target, damping, kind_left, kind_right,
    u_send, u_recv, side_send, side_recv, coef_side, coef_send, coef_recv,
):
    space = lax.axis_index("space")
    design = lax.axis_index("design")
    width_y, width_z = u_ref.shape[2], u_ref.shape[3]
    wide = 3 * rows
    own = slice(rows, 2 * rows)
    lower = slice(0, rows)
    upper = slice(2 * rows, wide)

    core = design % 2
    ring = (design // 2) % 4
    pair = design // 8
    primal = design == 0
    has_left = space > 0
    has_right = space < slabs - 1
    relay = core == 0
    to_partner = relay
    to_pair = relay & (pair == 0)
    to_next = relay & (pair == 0) & (ring < 2)
    children = (
        (to_next, design + 2),
        (primal, design + 6),
        (to_pair, design + 8),
        (to_partner, design + 1),
    )
    last = ring // 3
    parent = core * (design - 1) + (1 - core) * (
        pair * (design - 8) + (1 - pair) * (1 - last) * (design - 2)
    )

    def remote(src, dst, send, recv, where):
        return pltpu.make_async_remote_copy(
            src_ref=src, dst_ref=dst, send_sem=send, recv_sem=recv, device_id=where, device_id_type=MESH
        )

    left = (space - 1, design)
    right = (space + 1, design)

    barrier = pltpu.get_barrier_semaphore()
    partners = [(has_left, left), (has_right, right), (design > 0, (space, parent))]
    partners += [(on, (space, child)) for on, child in children]
    expected = jnp.int32(0)
    for on, where in partners:
        expected = expected + on.astype(jnp.int32)

        @pl.when(on)
        def _(where=where):
            pl.semaphore_signal(barrier, inc=1, device_id=where, device_id_type=MESH)

    pl.semaphore_wait(barrier, expected)

    def u_copies(step, k):
        src, first = (u_ref, 0) if step == 0 else (level.at[step, 0], rows)
        low, high = k, rows - 1 - k
        return (
            remote(
                src.at[:, pl.ds(first + low, 1)], level.at[step, 0, :, pl.ds(2 * rows + low, 1)],
                u_send.at[step, 0, k], u_recv.at[step, 1, k], left,
            ),
            remote(
                src.at[:, pl.ds(first + high, 1)], level.at[step, 0, :, pl.ds(high, 1)],
                u_send.at[step, 1, k], u_recv.at[step, 0, k], right,
            ),
        )

    kind_copies = (
        remote(kind_ref, kind_right, side_send.at[0], side_recv.at[1], left),
        remote(kind_ref, kind_left, side_send.at[1], side_recv.at[0], right),
    )
    source_copies = (
        remote(source_ref, target.at[:, upper], side_send.at[2], side_recv.at[3], left),
        remote(source_ref, target.at[:, lower], side_send.at[3], side_recv.at[2], right),
    )

    def coef_side_copies(step, k):
        low, high = k, rows - 1 - k
        return (
            remote(
                coef.at[step, :, pl.ds(rows + low, 1)], coef.at[step, :, pl.ds(2 * rows + low, 1)],
                coef_side.at[step, 0, k], coef_recv.at[step, 2 * rows + low], left,
            ),
            remote(
                coef.at[step, :, pl.ds(rows + high, 1)], coef.at[step, :, pl.ds(high, 1)],
                coef_side.at[step, 1, k], coef_recv.at[step, high], right,
            ),
        )

    def tree_copy(step, child, row):
        where = coef.at[step, :, pl.ds(row, 1)]
        return remote(
            where, where, coef_send.at[step, child, row], coef_recv.at[step, row], (space, children[child][1])
        )

    sides = (has_left, has_right)

    def on_sides(copies, action, also=None):
        for on, copy in zip(sides, copies):

            @pl.when(on if also is None else on & also)
            def _(copy=copy):
                action(copy)

    def recv_sides(copies, also=None):
        for on, copy in zip(sides, copies[::-1]):

            @pl.when(on if also is None else on & also)
            def _(copy=copy):
                copy.wait_recv()

    def start(copy):
        copy.start()

    def wait_send(copy):
        copy.wait_send()

    def forward(step, row, action):
        for child, (on, _) in enumerate(children):

            @pl.when(on)
            def _(child=child):
                action(tree_copy(step, child, row))

    def each_row(body):
        def one(k, carry):
            body(k)
            return carry

        lax.fori_loop(0, rows, one, 0)

    def side_rows(body):
        def both(k):
            @pl.when(has_left)
            def _():
                body(rows - 1 - k)

            @pl.when(has_right)
            def _():
                body(2 * rows + k)

        each_row(both)

    def leave(step):
        primal_coefficients(step)

        @pl.when(primal)
        def _():
            each_row(lambda k: on_sides(coef_side_copies(step, k), start))
            each_row(lambda k: forward(step, rows + k, start))

        each_row(lambda k: on_sides(u_copies(step, k), start))

    def relay_coefficients(step):
        def take(row):
            tree_copy(step, 0, row).wait_recv()
            forward(step, row, start)

        @pl.when(design > 0)
        def _():
            each_row(lambda k: take(rows + k))

        side_rows(take)

    def primal_coefficients(step):
        @pl.when(primal)
        def _():
            def row(r, carry):
                if step == 0:
                    p0, p1, p4 = u_ref[0, r], u_ref[1, r], u_ref[4, r]
                else:
                    p0, p1, p4 = (level[step, 0, f, rows + r] for f in (0, 1, 4))
                coef[step, 0, rows + r] = jnp.exp(0.5 * jnp.tanh(p4 - 0.5 * p0)) - 1.0
                coef[step, 1, rows + r] = jnp.tanh(p1)
                return carry

            lax.fori_loop(0, rows, row, 0)

    def blank(step):
        @pl.when(space == 0)
        def _():
            level[step, 0, :, lower] = jnp.zeros((FIELDS, rows, width_y, width_z), jnp.float32)
            coef[step, :, lower] = jnp.zeros((2, rows, width_y, width_z), jnp.float32)

        @pl.when(space == slabs - 1)
        def _():
            level[step, 0, :, upper] = jnp.zeros((FIELDS, rows, width_y, width_z), jnp.float32)
            coef[step, :, upper] = jnp.zeros((2, rows, width_y, width_z), jnp.float32)

    row_y = lax.broadcasted_iota(jnp.int32, (width_y, width_z), 0)
    row_z = lax.broadcasted_iota(jnp.int32, (width_y, width_z), 1)
    first_y, last_y = row_y == 0, row_y == width_y - 1
    first_z, last_z = row_z == 0, row_z == width_z - 1

    def shifts(plane):
        return (
            pltpu.roll(plane, 1, 0),
            pltpu.roll(plane, width_y - 1, 0),
            pltpu.roll(plane, 1, 1),
            pltpu.roll(plane, width_z - 1, 1),
        )

    edges = (first_y, last_y, first_z, last_z)

    def weights(step):
        def row(r, carry):
            centre = 1.0 + coef[step, 0, r]
            below = 0.5 * (centre + 1.0 + coef[step, 0, r - 1])
            above = 0.5 * (centre + 1.0 + coef[step, 0, r + 1])
            upwind = 1.0 + coef[step, 1, r]
            diagonal = damping[r] + upwind + below + above
            grid_row = space * rows + r - rows
            weight[0, r] = jnp.where(grid_row == 0, 0.0, below + upwind)
            weight[1, r] = jnp.where(grid_row == slabs * rows - 1, 0.0, above)
            for k, (near, edge) in enumerate(zip(shifts(centre), edges)):
                face = 0.5 * (centre + jnp.where(edge, 1.0, near))
                diagonal = diagonal + face
                weight[2 + k, r] = jnp.where(edge, 0.0, face)
            weight[6, r] = 1.0 / diagonal
            return carry

        lax.fori_loop(1, wide - 1, row, 0)

    def relax_row(src, dst, r, shift):
        planes = [src[f, r] for f in range(FIELDS)]
        for f in range(FIELDS):
            total = target[f, r] + weight[0, r] * src[f, r - 1] + weight[1, r] * src[f, r + 1]
            for k, near in enumerate(shifts(planes[f])):
                total = total + weight[2 + k, r] * near
            for h in range(FIELDS):
                total = total - coupling_ref[f, h] * planes[h]
            dst[f, r - shift] = total * weight[6, r]

    def sweep_own(step, stage):
        src, shift = level.at[step, stage - 1], 0
        if stage < SWEEPS:
            dst = level.at[step, stage]
        elif step < PSTEPS - 1:
            dst = level.at[step + 1, 0]
        else:
            dst, shift = out_ref, rows

        each_row(lambda k: relax_row(src, dst, rows + k, shift))

    def sweep_halo(step, k):
        def one(i, carry):
            stage, side = 1 + i // 2, i % 2
            out = k + 1 - stage
            r = rows - out + side * (rows - 1 + 2 * out)
            relax_row(level.at[step, stage - 1], level.at[step, stage], r, 0)
            return carry

        lax.fori_loop(0, 2 * k, one, 0)

    def spread_kinds(kinds, first):
        pick_b = lax.broadcasted_iota(jnp.int32, (width_z // ZB, width_z), 0)
        pick_z = lax.broadcasted_iota(jnp.int32, (width_z // ZB, width_z), 1)
        inside = (pick_z >= pick_b * ZB) & (pick_z < pick_b * ZB + ZB)
        for r in range(rows):
            cells = lax.dot_general(
                kinds[r].astype(jnp.float32), inside.astype(jnp.float32), (((0,), (0,)), ((), ())),
                preferred_element_type=jnp.float32,
            )
            damping[first + r] = 0.8 + jnp.where(cells == 1.0, 2.2, 0.0) + jnp.where(cells == 2.0, 0.7, 0.0)

    on_sides(kind_copies, start)
    leave(0)
    on_sides(source_copies, start, primal)

    blank(0)
    level[0, 0, :, own] = u_ref[...]

    @pl.when(primal)
    def _():
        target[:, own] = source_ref[...]

        @pl.when(space == 0)
        def _():
            target[:, lower] = jnp.zeros((FIELDS, rows, width_y, width_z), jnp.float32)

        @pl.when(space == slabs - 1)
        def _():
            target[:, upper] = jnp.zeros((FIELDS, rows, width_y, width_z), jnp.float32)

    @pl.when(design > 0)
    def _():
        tangents, count = points_ref.shape
        mine = lax.broadcasted_iota(jnp.int32, (tangents, count), 0) == design - 1
        points = jnp.sum(jnp.where(mine, points_ref[...], 0), axis=0, keepdims=True)
        shapes = jnp.concatenate(
            [
                jnp.sum(jnp.where(mine, shapes_ref[f], 0.0), axis=0, keepdims=True)
                for f in range(FIELDS)
            ],
            axis=0,
        )

        def row(r, carry):
            cell = (space * rows + r - rows) * width_z + lax.broadcasted_iota(
                jnp.int32, (width_z, count), 0
            )
            hit = (points == cell).astype(jnp.float32)
            wall = lax.dot_general(
                shapes, hit, (((1,), (1,)), ((), ())),
                precision=lax.Precision.HIGHEST, preferred_element_type=jnp.float32,
            )
            for f in range(FIELDS):
                line = jnp.broadcast_to(wall[f : f + 1], (width_y, width_z))
                target[f, r] = jnp.where(first_y, line, 0.0)
            return carry

        lax.fori_loop(0, wide, row, 0)

    spread_kinds(kind_ref, rows)

    for step in range(PSTEPS):
        if step > 0:
            leave(step)
            blank(step)

        relay_coefficients(step)

        if step == 0:
            recv_sides(kind_copies)

            @pl.when(has_left)
            def _():
                spread_kinds(kind_left, 0)

            @pl.when(has_right)
            def _():
                spread_kinds(kind_right, 2 * rows)

            @pl.when(space == 0)
            def _():
                damping[lower] = jnp.zeros((rows, width_y, width_z), jnp.float32)

            @pl.when(space == slabs - 1)
            def _():
                damping[upper] = jnp.zeros((rows, width_y, width_z), jnp.float32)

        weights(step)
        if step == 0:
            recv_sides(source_copies, primal)
        for k in range(SWEEPS):
            recv_sides(u_copies(step, k))
            if k > 0:
                sweep_halo(step, k)
            sweep_own(step, k + 1)

    on_sides(kind_copies, wait_send)
    on_sides(source_copies, wait_send, primal)
    for step in range(PSTEPS):
        each_row(lambda k: on_sides(u_copies(step, k), wait_send))

        @pl.when(primal)
        def _():
            each_row(lambda k: on_sides(coef_side_copies(step, k), wait_send))

        each_row(lambda k: forward(step, rows + k, wait_send))
        side_rows(lambda row: forward(step, row, wait_send))


def shards(states, source, cell_kind, wall_points, point_shape, coupling):
    member_state = states[0]
    fields, rows, width_y, width_z = member_state.shape
    slabs = lax.axis_size("space")
    kinds = jnp.transpose(cell_kind, (0, 2, 1))
    shapes = jnp.transpose(point_shape, (2, 0, 1))
    vmem = pl.BlockSpec(memory_space=pltpu.VMEM)
    wide = 3 * rows
    out = pl.pallas_call(
        functools.partial(kernel, slabs, rows),
        name="sweeps",
        out_shape=pltpu.VMEM(member_state.shape, jnp.float32),
        in_specs=[vmem] * 5 + [pl.BlockSpec(memory_space=pltpu.SMEM)],
        out_specs=vmem,
        scratch_shapes=[
            pltpu.VMEM((PSTEPS, SWEEPS, fields, wide, width_y, width_z), jnp.float32),
            pltpu.VMEM((PSTEPS, 2, wide, width_y, width_z), jnp.float32),
            pltpu.VMEM((7, wide, width_y, width_z), jnp.float32),
            pltpu.VMEM((fields, wide, width_y, width_z), jnp.float32),
            pltpu.VMEM((wide, width_y, width_z), jnp.float32),
            pltpu.VMEM(kinds.shape, jnp.int32),
            pltpu.VMEM(kinds.shape, jnp.int32),
            pltpu.SemaphoreType.DMA((PSTEPS, 2, rows)),
            pltpu.SemaphoreType.DMA((PSTEPS, 2, rows)),
            pltpu.SemaphoreType.DMA((4,)),
            pltpu.SemaphoreType.DMA((4,)),
            pltpu.SemaphoreType.DMA((PSTEPS, 2, rows)),
            pltpu.SemaphoreType.DMA((PSTEPS, 4, wide)),
            pltpu.SemaphoreType.DMA((PSTEPS, wide)),
        ],
        compiler_params=pltpu.CompilerParams(collective_id=0, has_side_effects=True),
    )(member_state, source, kinds, wall_points, shapes, coupling)
    return out[None]


def solution(mesh):
    in_specs = (
        P("design", None, "space", None, None),
        P(None, "space", None, None),
        P("space", None, None),
        P(),
        P(),
        P(),
    )
    out_specs = P("design", None, "space", None, None)
    return jax.shard_map(shards, mesh=mesh, in_specs=in_specs, out_specs=out_specs, check_vma=False)
```

```python
import functools

import jax
import jax.numpy as jnp
from jax import lax
from jax.experimental import pallas as pl
from jax.experimental.pallas import tpu as pltpu
from jax.sharding import PartitionSpec as P

ZB = 8
SWEEPS = 4
PSTEPS = 2
FIELDS = 5
MESH = pl.DeviceIdType.MESH


def kernel(
    slabs, rows,
    u_ref, source_ref, kind_ref, points_ref, shapes_ref, coupling_ref,
    out_ref,
    level, coef, weight, target, damping, kind_left, kind_right,
    u_send, u_recv, side_send, side_recv, coef_side, coef_send, coef_recv,
):
    space = lax.axis_index("space")
    design = lax.axis_index("design")
    width_y, width_z = u_ref.shape[2], u_ref.shape[3]
    wide = 3 * rows
    own = slice(rows, 2 * rows)
    lower = slice(0, rows)
    upper = slice(2 * rows, wide)

    core = design % 2
    ring = (design // 2) % 4
    pair = design // 8
    primal = design == 0
    has_left = space > 0
    has_right = space < slabs - 1
    relay = core == 0
    to_partner = relay
    to_pair = relay & (pair == 0)
    to_next = relay & (pair == 0) & (ring < 2)
    children = (
        (to_next, design + 2),
        (primal, design + 6),
        (to_pair, design + 8),
        (to_partner, design + 1),
    )
    last = ring // 3
    parent = core * (design - 1) + (1 - core) * (
        pair * (design - 8) + (1 - pair) * (1 - last) * (design - 2)
    )

    def remote(src, dst, send, recv, where):
        return pltpu.make_async_remote_copy(
            src_ref=src, dst_ref=dst, send_sem=send, recv_sem=recv, device_id=where, device_id_type=MESH
        )

    left = (space - 1, design)
    right = (space + 1, design)

    barrier = pltpu.get_barrier_semaphore()
    partners = [(has_left, left), (has_right, right), (design > 0, (space, parent))]
    partners += [(on, (space, child)) for on, child in children]
    expected = jnp.int32(0)
    for on, where in partners:
        expected = expected + on.astype(jnp.int32)

        @pl.when(on)
        def _(where=where):
            pl.semaphore_signal(barrier, inc=1, device_id=where, device_id_type=MESH)

    pl.semaphore_wait(barrier, expected)

    def u_copies(step, k):
        src, first = (u_ref, 0) if step == 0 else (level.at[step, 0], rows)
        low, high = k, rows - 1 - k
        return (
            remote(
                src.at[:, pl.ds(first + low, 1)], level.at[step, 0, :, pl.ds(2 * rows + low, 1)],
                u_send.at[step, 0, k], u_recv.at[step, 1, k], left,
            ),
            remote(
                src.at[:, pl.ds(first + high, 1)], level.at[step, 0, :, pl.ds(high, 1)],
                u_send.at[step, 1, k], u_recv.at[step, 0, k], right,
            ),
        )

    kind_copies = (
        remote(kind_ref, kind_right, side_send.at[0], side_recv.at[1], left),
        remote(kind_ref, kind_left, side_send.at[1], side_recv.at[0], right),
    )
    def source_copies(k):
        low, high = k, rows - 1 - k
        return (
            remote(
                source_ref.at[:, pl.ds(low, 1)], target.at[:, pl.ds(2 * rows + low, 1)],
                side_send.at[2 + 2 * k], side_recv.at[3 + 2 * k], left,
            ),
            remote(
                source_ref.at[:, pl.ds(high, 1)], target.at[:, pl.ds(high, 1)],
                side_send.at[3 + 2 * k], side_recv.at[2 + 2 * k], right,
            ),
        )

    def coef_side_copies(step, k):
        low, high = k, rows - 1 - k
        return (
            remote(
                coef.at[step, :, pl.ds(rows + low, 1)], coef.at[step, :, pl.ds(2 * rows + low, 1)],
                coef_side.at[step, 0, k], coef_recv.at[step, 2 * rows + low], left,
            ),
            remote(
                coef.at[step, :, pl.ds(rows + high, 1)], coef.at[step, :, pl.ds(high, 1)],
                coef_side.at[step, 1, k], coef_recv.at[step, high], right,
            ),
        )

    def tree_copy(step, child, row):
        where = coef.at[step, :, pl.ds(row, 1)]
        return remote(
            where, where, coef_send.at[step, child, row], coef_recv.at[step, row], (space, children[child][1])
        )

    sides = (has_left, has_right)

    def on_sides(copies, action, also=None):
        for on, copy in zip(sides, copies):

            @pl.when(on if also is None else on & also)
            def _(copy=copy):
                action(copy)

    def recv_sides(copies, also=None):
        for on, copy in zip(sides, copies[::-1]):

            @pl.when(on if also is None else on & also)
            def _(copy=copy):
                copy.wait_recv()

    def start(copy):
        copy.start()

    def wait_send(copy):
        copy.wait_send()

    def forward(step, row, action):
        for child, (on, _) in enumerate(children):

            @pl.when(on)
            def _(child=child):
                action(tree_copy(step, child, row))

    def each_row(body):
        def one(k, carry):
            body(k)
            return carry

        lax.fori_loop(0, rows, one, 0)

    def side_rows(body):
        def both(k):
            @pl.when(has_left)
            def _():
                body(rows - 1 - k)

            @pl.when(has_right)
            def _():
                body(2 * rows + k)

        each_row(both)

    def leave(step):
        primal_coefficients(step)

        @pl.when(primal)
        def _():
            each_row(lambda k: on_sides(coef_side_copies(step, k), start))
            each_row(lambda k: forward(step, rows + k, start))

        each_row(lambda k: on_sides(u_copies(step, k), start))

    root = relay & (pair == 0)

    def take(step, row):
        tree_copy(step, 0, row).wait_recv()
        forward(step, row, start)

    def relay_coefficients(step):
        @pl.when(design > 0)
        def _():
            each_row(lambda k: take(step, rows + k))

        @pl.when(root)
        def _():
            side_rows(lambda row: take(step, row))

    def late_coefficients(step, k):
        @pl.when(has_left & (design > 0) & ~root)
        def _():
            take(step, rows - 1 - k)

        @pl.when(has_right & (design > 0) & ~root)
        def _():
            take(step, 2 * rows + k)

    def primal_coefficients(step):
        @pl.when(primal)
        def _():
            def row(r, carry):
                if step == 0:
                    p0, p1, p4 = u_ref[0, r], u_ref[1, r], u_ref[4, r]
                else:
                    p0, p1, p4 = (level[step, 0, f, rows + r] for f in (0, 1, 4))
                coef[step, 0, rows + r] = jnp.exp(0.5 * jnp.tanh(p4 - 0.5 * p0)) - 1.0
                coef[step, 1, rows + r] = jnp.tanh(p1)
                return carry

            lax.fori_loop(0, rows, row, 0)

    def blank(step):
        @pl.when(space == 0)
        def _():
            level[step, 0, :, lower] = jnp.zeros((FIELDS, rows, width_y, width_z), jnp.float32)
            coef[step, :, lower] = jnp.zeros((2, rows, width_y, width_z), jnp.float32)

        @pl.when(space == slabs - 1)
        def _():
            level[step, 0, :, upper] = jnp.zeros((FIELDS, rows, width_y, width_z), jnp.float32)
            coef[step, :, upper] = jnp.zeros((2, rows, width_y, width_z), jnp.float32)

    row_y = lax.broadcasted_iota(jnp.int32, (width_y, width_z), 0)
    row_z = lax.broadcasted_iota(jnp.int32, (width_y, width_z), 1)
    first_y, last_y = row_y == 0, row_y == width_y - 1
    first_z, last_z = row_z == 0, row_z == width_z - 1

    def shifts(plane):
        return (
            pltpu.roll(plane, 1, 0),
            pltpu.roll(plane, width_y - 1, 0),
            pltpu.roll(plane, 1, 1),
            pltpu.roll(plane, width_z - 1, 1),
        )

    edges = (first_y, last_y, first_z, last_z)

    def weight_row(step, r):
        centre = 1.0 + coef[step, 0, r]
        below = 0.5 * (centre + 1.0 + coef[step, 0, r - 1])
        above = 0.5 * (centre + 1.0 + coef[step, 0, r + 1])
        upwind = 1.0 + coef[step, 1, r]
        diagonal = damping[r] + upwind + below + above
        grid_row = space * rows + r - rows
        weight[0, r] = jnp.where(grid_row == 0, 0.0, below + upwind)
        weight[1, r] = jnp.where(grid_row == slabs * rows - 1, 0.0, above)
        for k, (near, edge) in enumerate(zip(shifts(centre), edges)):
            face = 0.5 * (centre + jnp.where(edge, 1.0, near))
            diagonal = diagonal + face
            weight[2 + k, r] = jnp.where(edge, 0.0, face)
        weight[6, r] = 1.0 / diagonal

    def weights(step, k):
        if k == 0:
            each_row(lambda i: weight_row(step, rows + i))
        else:

            def one(side, carry):
                weight_row(step, rows - k + side * (rows - 1 + 2 * k))
                return carry

            lax.fori_loop(0, 2, one, 0)

    def relax_row(src, dst, r, shift):
        planes = [src[f, r] for f in range(FIELDS)]
        for f in range(FIELDS):
            total = target[f, r] + weight[0, r] * src[f, r - 1] + weight[1, r] * src[f, r + 1]
            for k, near in enumerate(shifts(planes[f])):
                total = total + weight[2 + k, r] * near
            for h in range(FIELDS):
                total = total - coupling_ref[f, h] * planes[h]
            dst[f, r - shift] = total * weight[6, r]

    def sweep_own(step, stage):
        src, shift = level.at[step, stage - 1], 0
        if stage < SWEEPS:
            dst = level.at[step, stage]
        elif step < PSTEPS - 1:
            dst = level.at[step + 1, 0]
        else:
            dst, shift = out_ref, rows

        each_row(lambda k: relax_row(src, dst, rows + k, shift))

    def sweep_halo(step, k):
        def one(i, carry):
            stage, side = 1 + i // 2, i % 2
            out = k + 1 - stage
            r = rows - out + side * (rows - 1 + 2 * out)
            relax_row(level.at[step, stage - 1], level.at[step, stage], r, 0)
            return carry

        lax.fori_loop(0, 2 * k, one, 0)

    def spread_kinds(kinds, first):
        pick_b = lax.broadcasted_iota(jnp.int32, (width_z // ZB, width_z), 0)
        pick_z = lax.broadcasted_iota(jnp.int32, (width_z // ZB, width_z), 1)
        inside = (pick_z >= pick_b * ZB) & (pick_z < pick_b * ZB + ZB)
        for r in range(rows):
            cells = lax.dot_general(
                kinds[r].astype(jnp.float32), inside.astype(jnp.float32), (((0,), (0,)), ((), ())),
                preferred_element_type=jnp.float32,
            )
            damping[first + r] = 0.8 + jnp.where(cells == 1.0, 2.2, 0.0) + jnp.where(cells == 2.0, 0.7, 0.0)

    on_sides(kind_copies, start)
    leave(0)
    for k in range(SWEEPS - 1):
        on_sides(source_copies(k), start, primal)

    blank(0)
    level[0, 0, :, own] = u_ref[...]

    @pl.when(primal)
    def _():
        target[:, own] = source_ref[...]

        @pl.when(space == 0)
        def _():
            target[:, lower] = jnp.zeros((FIELDS, rows, width_y, width_z), jnp.float32)

        @pl.when(space == slabs - 1)
        def _():
            target[:, upper] = jnp.zeros((FIELDS, rows, width_y, width_z), jnp.float32)

    @pl.when(design > 0)
    def _():
        tangents, count = points_ref.shape
        mine = lax.broadcasted_iota(jnp.int32, (tangents, count), 0) == design - 1
        points = jnp.sum(jnp.where(mine, points_ref[...], 0), axis=0, keepdims=True)
        shapes = jnp.concatenate(
            [
                jnp.sum(jnp.where(mine, shapes_ref[f], 0.0), axis=0, keepdims=True)
                for f in range(FIELDS)
            ],
            axis=0,
        )

        def row(r, carry):
            cell = (space * rows + r - rows) * width_z + lax.broadcasted_iota(
                jnp.int32, (width_z, count), 0
            )
            hit = (points == cell).astype(jnp.float32)
            wall = lax.dot_general(
                shapes, hit, (((1,), (1,)), ((), ())),
                precision=lax.Precision.HIGHEST, preferred_element_type=jnp.float32,
            )
            for f in range(FIELDS):
                line = jnp.broadcast_to(wall[f : f + 1], (width_y, width_z))
                target[f, r] = jnp.where(first_y, line, 0.0)
            return carry

        lax.fori_loop(0, wide, row, 0)

    spread_kinds(kind_ref, rows)

    for step in range(PSTEPS):
        if step > 0:
            leave(step)
            blank(step)

        relay_coefficients(step)

        if step == 0:
            recv_sides(kind_copies)

            @pl.when(has_left)
            def _():
                spread_kinds(kind_left, 0)

            @pl.when(has_right)
            def _():
                spread_kinds(kind_right, 2 * rows)

            @pl.when(space == 0)
            def _():
                damping[lower] = jnp.zeros((rows, width_y, width_z), jnp.float32)

            @pl.when(space == slabs - 1)
            def _():
                damping[upper] = jnp.zeros((rows, width_y, width_z), jnp.float32)

        for k in range(SWEEPS):
            late_coefficients(step, k)
            weights(step, k)
            recv_sides(u_copies(step, k))
            if k > 0:
                if step == 0:
                    recv_sides(source_copies(k - 1), primal)
                sweep_halo(step, k)
            sweep_own(step, k + 1)

    on_sides(kind_copies, wait_send)
    for k in range(SWEEPS - 1):
        on_sides(source_copies(k), wait_send, primal)
    for step in range(PSTEPS):
        each_row(lambda k: on_sides(u_copies(step, k), wait_send))

        @pl.when(primal)
        def _():
            each_row(lambda k: on_sides(coef_side_copies(step, k), wait_send))

        each_row(lambda k: forward(step, rows + k, wait_send))
        side_rows(lambda row: forward(step, row, wait_send))


def shards(states, source, cell_kind, wall_points, point_shape, coupling):
    member_state = states[0]
    fields, rows, width_y, width_z = member_state.shape
    slabs = lax.axis_size("space")
    kinds = jnp.transpose(cell_kind, (0, 2, 1))
    shapes = jnp.transpose(point_shape, (2, 0, 1))
    vmem = pl.BlockSpec(memory_space=pltpu.VMEM)
    wide = 3 * rows
    out = pl.pallas_call(
        functools.partial(kernel, slabs, rows),
        name="sweeps",
        out_shape=pltpu.VMEM(member_state.shape, jnp.float32),
        in_specs=[vmem] * 5 + [pl.BlockSpec(memory_space=pltpu.SMEM)],
        out_specs=vmem,
        scratch_shapes=[
            pltpu.VMEM((PSTEPS, SWEEPS, fields, wide, width_y, width_z), jnp.float32),
            pltpu.VMEM((PSTEPS, 2, wide, width_y, width_z), jnp.float32),
            pltpu.VMEM((7, wide, width_y, width_z), jnp.float32),
            pltpu.VMEM((fields, wide, width_y, width_z), jnp.float32),
            pltpu.VMEM((wide, width_y, width_z), jnp.float32),
            pltpu.VMEM(kinds.shape, jnp.int32),
            pltpu.VMEM(kinds.shape, jnp.int32),
            pltpu.SemaphoreType.DMA((PSTEPS, 2, rows)),
            pltpu.SemaphoreType.DMA((PSTEPS, 2, rows)),
            pltpu.SemaphoreType.DMA((2 * rows,)),
            pltpu.SemaphoreType.DMA((2 * rows,)),
            pltpu.SemaphoreType.DMA((PSTEPS, 2, rows)),
            pltpu.SemaphoreType.DMA((PSTEPS, 4, wide)),
            pltpu.SemaphoreType.DMA((PSTEPS, wide)),
        ],
        compiler_params=pltpu.CompilerParams(collective_id=0, has_side_effects=True),
    )(member_state, source, kinds, wall_points, shapes, coupling)
    return out[None]


def solution(mesh):
    in_specs = (
        P("design", None, "space", None, None),
        P(None, "space", None, None),
        P("space", None, None),
        P(),
        P(),
        P(),
    )
    out_specs = P("design", None, "space", None, None)
    return jax.shard_map(shards, mesh=mesh, in_specs=in_specs, out_specs=out_specs, check_vma=False)
```

```python
import functools

import jax
import jax.numpy as jnp
from jax import lax
from jax.experimental import pallas as pl
from jax.experimental.pallas import tpu as pltpu
from jax.sharding import PartitionSpec as P

ZB = 8
SWEEPS = 4
PSTEPS = 2
FIELDS = 5
MESH = pl.DeviceIdType.MESH


def kernel(
    slabs, rows,
    u_ref, source_ref, kind_ref, points_ref, shapes_ref, coupling_ref,
    out_ref,
    level, coef, weight, target, damping, kind_left, kind_right,
    u_send, u_recv, side_send, side_recv, coef_side, coef_send, coef_recv,
):
    space = lax.axis_index("space")
    design = lax.axis_index("design")
    width_y, width_z = u_ref.shape[2], u_ref.shape[3]
    wide = 3 * rows
    own = slice(rows, 2 * rows)
    lower = slice(0, rows)
    upper = slice(2 * rows, wide)

    core = design % 2
    ring = (design // 2) % 4
    pair = design // 8
    primal = design == 0
    has_left = space > 0
    has_right = space < slabs - 1
    relay = core == 0
    to_partner = relay
    to_pair = relay & (pair == 0)
    to_next = relay & (pair == 0) & (ring < 2)
    children = (
        (to_next, design + 2),
        (primal, design + 6),
        (to_pair, design + 8),
        (to_partner, design + 1),
    )
    last = ring // 3
    parent = core * (design - 1) + (1 - core) * (
        pair * (design - 8) + (1 - pair) * (1 - last) * (design - 2)
    )

    def remote(src, dst, send, recv, where):
        return pltpu.make_async_remote_copy(
            src_ref=src, dst_ref=dst, send_sem=send, recv_sem=recv, device_id=where, device_id_type=MESH
        )

    left = (space - 1, design)
    right = (space + 1, design)

    barrier = pltpu.get_barrier_semaphore()
    partners = [(has_left, left), (has_right, right), (design > 0, (space, parent))]
    partners += [(on, (space, child)) for on, child in children]
    expected = jnp.int32(0)
    for on, where in partners:
        expected = expected + on.astype(jnp.int32)

        @pl.when(on)
        def _(where=where):
            pl.semaphore_signal(barrier, inc=1, device_id=where, device_id_type=MESH)

    pl.semaphore_wait(barrier, expected)

    def u_copies(step, k):
        src, first = (u_ref, 0) if step == 0 else (level.at[step, 0], rows)
        low, high = k, rows - 1 - k
        return (
            remote(
                src.at[:, pl.ds(first + low, 1)], level.at[step, 0, :, pl.ds(2 * rows + low, 1)],
                u_send.at[step, 0, k], u_recv.at[step, 1, k], left,
            ),
            remote(
                src.at[:, pl.ds(first + high, 1)], level.at[step, 0, :, pl.ds(high, 1)],
                u_send.at[step, 1, k], u_recv.at[step, 0, k], right,
            ),
        )

    kind_copies = (
        remote(kind_ref, kind_right, side_send.at[0], side_recv.at[1], left),
        remote(kind_ref, kind_left, side_send.at[1], side_recv.at[0], right),
    )
    def source_copies(k):
        low, high = k, rows - 1 - k
        return (
            remote(
                source_ref.at[:, pl.ds(low, 1)], target.at[:, pl.ds(2 * rows + low, 1)],
                side_send.at[2 + 2 * k], side_recv.at[3 + 2 * k], left,
            ),
            remote(
                source_ref.at[:, pl.ds(high, 1)], target.at[:, pl.ds(high, 1)],
                side_send.at[3 + 2 * k], side_recv.at[2 + 2 * k], right,
            ),
        )

    def needed(last):
        return pl.ds(0, 1 if last else 2)

    def coef_side_copies(step, k, last):
        low, high = k, rows - 1 - k
        kept = needed(last)
        return (
            remote(
                coef.at[step, kept, pl.ds(rows + low, 1)], coef.at[step, kept, pl.ds(2 * rows + low, 1)],
                coef_side.at[step, 0, k], coef_recv.at[step, 2 * rows + low], left,
            ),
            remote(
                coef.at[step, kept, pl.ds(rows + high, 1)], coef.at[step, kept, pl.ds(high, 1)],
                coef_side.at[step, 1, k], coef_recv.at[step, high], right,
            ),
        )

    def tree_copy(step, child, row, last=False):
        where = coef.at[step, needed(last), pl.ds(row, 1)]
        return remote(
            where, where, coef_send.at[step, child, row], coef_recv.at[step, row], (space, children[child][1])
        )

    sides = (has_left, has_right)

    def on_sides(copies, action, also=None):
        for on, copy in zip(sides, copies):

            @pl.when(on if also is None else on & also)
            def _(copy=copy):
                action(copy)

    def recv_sides(copies, also=None):
        for on, copy in zip(sides, copies[::-1]):

            @pl.when(on if also is None else on & also)
            def _(copy=copy):
                copy.wait_recv()

    def start(copy):
        copy.start()

    def wait_send(copy):
        copy.wait_send()

    def forward(step, row, action, last=False):
        for child, (on, _) in enumerate(children):

            @pl.when(on)
            def _(child=child):
                action(tree_copy(step, child, row, last))

    def each_row(body):
        def one(k, carry):
            body(k)
            return carry

        lax.fori_loop(0, rows, one, 0)

    def but_last(body):
        def one(k, carry):
            body(k, False)
            return carry

        lax.fori_loop(0, rows - 1, one, 0)
        body(rows - 1, True)

    def side_rows(body):
        def both(k, last):
            @pl.when(has_left)
            def _():
                body(rows - 1 - k, last)

            @pl.when(has_right)
            def _():
                body(2 * rows + k, last)

        but_last(both)

    def leave(step):
        primal_coefficients(step)

        @pl.when(primal)
        def _():
            but_last(lambda k, last: on_sides(coef_side_copies(step, k, last), start))
            each_row(lambda k: forward(step, rows + k, start))

        leave_states(step, design != 1)

    def leave_states(step, who):
        @pl.when(who)
        def _():
            each_row(lambda k: on_sides(u_copies(step, k), start))

    root = relay & (pair == 0)

    def take(step, row, last=False):
        tree_copy(step, 0, row, last).wait_recv()
        forward(step, row, start, last)

    def relay_coefficients(step):
        @pl.when(design > 0)
        def _():
            each_row(lambda k: take(step, rows + k))

        leave_states(step, design == 1)

        @pl.when(root)
        def _():
            side_rows(lambda row, last: take(step, row, last))

    def late_coefficients(step, k):
        @pl.when(has_left & (design > 0) & ~root)
        def _():
            take(step, rows - 1 - k, k == rows - 1)

        @pl.when(has_right & (design > 0) & ~root)
        def _():
            take(step, 2 * rows + k, k == rows - 1)

    def primal_coefficients(step):
        @pl.when(primal)
        def _():
            def row(r, carry):
                if step == 0:
                    p0, p1, p4 = u_ref[0, r], u_ref[1, r], u_ref[4, r]
                else:
                    p0, p1, p4 = (level[step, 0, f, rows + r] for f in (0, 1, 4))
                coef[step, 0, rows + r] = jnp.exp(0.5 * jnp.tanh(p4 - 0.5 * p0)) - 1.0
                coef[step, 1, rows + r] = jnp.tanh(p1)
                return carry

            lax.fori_loop(0, rows, row, 0)

    def blank(step):
        @pl.when(space == 0)
        def _():
            level[step, 0, :, lower] = jnp.zeros((FIELDS, rows, width_y, width_z), jnp.float32)
            coef[step, :, lower] = jnp.zeros((2, rows, width_y, width_z), jnp.float32)

        @pl.when(space == slabs - 1)
        def _():
            level[step, 0, :, upper] = jnp.zeros((FIELDS, rows, width_y, width_z), jnp.float32)
            coef[step, :, upper] = jnp.zeros((2, rows, width_y, width_z), jnp.float32)

    row_y = lax.broadcasted_iota(jnp.int32, (width_y, width_z), 0)
    row_z = lax.broadcasted_iota(jnp.int32, (width_y, width_z), 1)
    first_y, last_y = row_y == 0, row_y == width_y - 1
    first_z, last_z = row_z == 0, row_z == width_z - 1

    def shifts(plane):
        return (
            pltpu.roll(plane, 1, 0),
            pltpu.roll(plane, width_y - 1, 0),
            pltpu.roll(plane, 1, 1),
            pltpu.roll(plane, width_z - 1, 1),
        )

    edges = (first_y, last_y, first_z, last_z)

    def weight_row(step, r):
        centre = 1.0 + coef[step, 0, r]
        below = 0.5 * (centre + 1.0 + coef[step, 0, r - 1])
        above = 0.5 * (centre + 1.0 + coef[step, 0, r + 1])
        upwind = 1.0 + coef[step, 1, r]
        diagonal = damping[r] + upwind + below + above
        grid_row = space * rows + r - rows
        weight[0, r] = jnp.where(grid_row == 0, 0.0, below + upwind)
        weight[1, r] = jnp.where(grid_row == slabs * rows - 1, 0.0, above)
        for k, (near, edge) in enumerate(zip(shifts(centre), edges)):
            face = 0.5 * (centre + jnp.where(edge, 1.0, near))
            diagonal = diagonal + face
            weight[2 + k, r] = jnp.where(edge, 0.0, face)
        weight[6, r] = 1.0 / diagonal

    def weights(step, k):
        if k == 0:
            each_row(lambda i: weight_row(step, rows + i))
        else:

            def one(side, carry):
                weight_row(step, rows - k + side * (rows - 1 + 2 * k))
                return carry

            lax.fori_loop(0, 2, one, 0)

    def relax_row(src, dst, r, shift):
        planes = [src[f, r] for f in range(FIELDS)]
        for f in range(FIELDS):
            total = target[f, r] + weight[0, r] * src[f, r - 1] + weight[1, r] * src[f, r + 1]
            for k, near in enumerate(shifts(planes[f])):
                total = total + weight[2 + k, r] * near
            for h in range(FIELDS):
                total = total - coupling_ref[f, h] * planes[h]
            dst[f, r - shift] = total * weight[6, r]

    def sweep_own(step, stage):
        src, shift = level.at[step, stage - 1], 0
        if stage < SWEEPS:
            dst = level.at[step, stage]
        elif step < PSTEPS - 1:
            dst = level.at[step + 1, 0]
        else:
            dst, shift = out_ref, rows

        each_row(lambda k: relax_row(src, dst, rows + k, shift))

    def sweep_halo(step, k):
        def one(i, carry):
            stage, side = 1 + i // 2, i % 2
            out = k + 1 - stage
            r = rows - out + side * (rows - 1 + 2 * out)
            relax_row(level.at[step, stage - 1], level.at[step, stage], r, 0)
            return carry

        lax.fori_loop(0, 2 * k, one, 0)

    def spread_kinds(kinds, first):
        pick_b = lax.broadcasted_iota(jnp.int32, (width_z // ZB, width_z), 0)
        pick_z = lax.broadcasted_iota(jnp.int32, (width_z // ZB, width_z), 1)
        inside = (pick_z >= pick_b * ZB) & (pick_z < pick_b * ZB + ZB)
        for r in range(rows):
            cells = lax.dot_general(
                kinds[r].astype(jnp.float32), inside.astype(jnp.float32), (((0,), (0,)), ((), ())),
                preferred_element_type=jnp.float32,
            )
            damping[first + r] = 0.8 + jnp.where(cells == 1.0, 2.2, 0.0) + jnp.where(cells == 2.0, 0.7, 0.0)

    on_sides(kind_copies, start)
    leave(0)
    for k in range(SWEEPS - 1):
        on_sides(source_copies(k), start, primal)

    blank(0)
    level[0, 0, :, own] = u_ref[...]

    @pl.when(primal)
    def _():
        target[:, own] = source_ref[...]

        @pl.when(space == 0)
        def _():
            target[:, lower] = jnp.zeros((FIELDS, rows, width_y, width_z), jnp.float32)

        @pl.when(space == slabs - 1)
        def _():
            target[:, upper] = jnp.zeros((FIELDS, rows, width_y, width_z), jnp.float32)

    @pl.when(design > 0)
    def _():
        tangents, count = points_ref.shape
        mine = lax.broadcasted_iota(jnp.int32, (tangents, count), 0) == design - 1
        points = jnp.sum(jnp.where(mine, points_ref[...], 0), axis=0, keepdims=True)
        shapes = jnp.concatenate(
            [
                jnp.sum(jnp.where(mine, shapes_ref[f], 0.0), axis=0, keepdims=True)
                for f in range(FIELDS)
            ],
            axis=0,
        )

        def row(r, carry):
            cell = (space * rows + r - rows) * width_z + lax.broadcasted_iota(
                jnp.int32, (width_z, count), 0
            )
            hit = (points == cell).astype(jnp.float32)
            wall = lax.dot_general(
                shapes, hit, (((1,), (1,)), ((), ())),
                precision=lax.Precision.HIGHEST, preferred_element_type=jnp.float32,
            )
            for f in range(FIELDS):
                line = jnp.broadcast_to(wall[f : f + 1], (width_y, width_z))
                target[f, r] = jnp.where(first_y, line, 0.0)
            return carry

        lax.fori_loop(0, wide, row, 0)

    spread_kinds(kind_ref, rows)

    for step in range(PSTEPS):
        if step > 0:
            leave(step)
            blank(step)

        relay_coefficients(step)

        if step == 0:
            recv_sides(kind_copies)

            @pl.when(has_left)
            def _():
                spread_kinds(kind_left, 0)

            @pl.when(has_right)
            def _():
                spread_kinds(kind_right, 2 * rows)

            @pl.when(space == 0)
            def _():
                damping[lower] = jnp.zeros((rows, width_y, width_z), jnp.float32)

            @pl.when(space == slabs - 1)
            def _():
                damping[upper] = jnp.zeros((rows, width_y, width_z), jnp.float32)

        for k in range(SWEEPS):
            late_coefficients(step, k)
            weights(step, k)
            recv_sides(u_copies(step, k))
            if k > 0:
                if step == 0:
                    recv_sides(source_copies(k - 1), primal)
                sweep_halo(step, k)
            sweep_own(step, k + 1)

    on_sides(kind_copies, wait_send)
    for k in range(SWEEPS - 1):
        on_sides(source_copies(k), wait_send, primal)
    for step in range(PSTEPS):
        each_row(lambda k: on_sides(u_copies(step, k), wait_send))

        @pl.when(primal)
        def _():
            but_last(lambda k, last: on_sides(coef_side_copies(step, k, last), wait_send))

        each_row(lambda k: forward(step, rows + k, wait_send))
        side_rows(lambda row, last: forward(step, row, wait_send, last))


def shards(states, source, cell_kind, wall_points, point_shape, coupling):
    member_state = states[0]
    fields, rows, width_y, width_z = member_state.shape
    slabs = lax.axis_size("space")
    kinds = jnp.transpose(cell_kind, (0, 2, 1))
    shapes = jnp.transpose(point_shape, (2, 0, 1))
    vmem = pl.BlockSpec(memory_space=pltpu.VMEM)
    wide = 3 * rows
    out = pl.pallas_call(
        functools.partial(kernel, slabs, rows),
        name="sweeps",
        out_shape=pltpu.VMEM(member_state.shape, jnp.float32),
        in_specs=[vmem] * 5 + [pl.BlockSpec(memory_space=pltpu.SMEM)],
        out_specs=vmem,
        scratch_shapes=[
            pltpu.VMEM((PSTEPS, SWEEPS, fields, wide, width_y, width_z), jnp.float32),
            pltpu.VMEM((PSTEPS, 2, wide, width_y, width_z), jnp.float32),
            pltpu.VMEM((7, wide, width_y, width_z), jnp.float32),
            pltpu.VMEM((fields, wide, width_y, width_z), jnp.float32),
            pltpu.VMEM((wide, width_y, width_z), jnp.float32),
            pltpu.VMEM(kinds.shape, jnp.int32),
            pltpu.VMEM(kinds.shape, jnp.int32),
            pltpu.SemaphoreType.DMA((PSTEPS, 2, rows)),
            pltpu.SemaphoreType.DMA((PSTEPS, 2, rows)),
            pltpu.SemaphoreType.DMA((2 * rows,)),
            pltpu.SemaphoreType.DMA((2 * rows,)),
            pltpu.SemaphoreType.DMA((PSTEPS, 2, rows)),
            pltpu.SemaphoreType.DMA((PSTEPS, 4, wide)),
            pltpu.SemaphoreType.DMA((PSTEPS, wide)),
        ],
        compiler_params=pltpu.CompilerParams(collective_id=0, has_side_effects=True),
    )(member_state, source, kinds, wall_points, shapes, coupling)
    return out[None]


def solution(mesh):
    in_specs = (
        P("design", None, "space", None, None),
        P(None, "space", None, None),
        P("space", None, None),
        P(),
        P(),
        P(),
    )
    out_specs = P("design", None, "space", None, None)
    return jax.shard_map(shards, mesh=mesh, in_specs=in_specs, out_specs=out_specs, check_vma=False)
```

```python
import functools

import jax
import jax.numpy as jnp
from jax import lax
from jax.experimental import pallas as pl
from jax.experimental.pallas import tpu as pltpu
from jax.sharding import PartitionSpec as P

ZB = 8
SWEEPS = 4
PSTEPS = 2
FIELDS = 5
MESH = pl.DeviceIdType.MESH


def kernel(
    slabs, rows,
    u_ref, source_ref, kind_ref, points_ref, shapes_ref, coupling_ref,
    out_ref,
    level, coef, weight, target, damping, kind_left, kind_right,
    u_send, u_recv, side_send, side_recv, coef_side, coef_send, coef_recv,
):
    space = lax.axis_index("space")
    design = lax.axis_index("design")
    width_y, width_z = u_ref.shape[2], u_ref.shape[3]
    wide = 3 * rows
    own = slice(rows, 2 * rows)
    lower = slice(0, rows)
    upper = slice(2 * rows, wide)

    core = design % 2
    ring = (design // 2) % 4
    pair = design // 8
    primal = design == 0
    has_left = space > 0
    has_right = space < slabs - 1
    relay = core == 0
    to_partner = relay
    to_pair = relay & (pair == 0)
    to_next = relay & (pair == 0) & (ring < 2)
    children = (
        (to_next, design + 2),
        (primal, design + 6),
        (to_pair, design + 8),
        (to_partner, design + 1),
    )
    last = ring // 3
    parent = core * (design - 1) + (1 - core) * (
        pair * (design - 8) + (1 - pair) * (1 - last) * (design - 2)
    )

    def remote(src, dst, send, recv, where):
        return pltpu.make_async_remote_copy(
            src_ref=src, dst_ref=dst, send_sem=send, recv_sem=recv, device_id=where, device_id_type=MESH
        )

    left = (space - 1, design)
    right = (space + 1, design)

    barrier = pltpu.get_barrier_semaphore()
    partners = [(has_left, left), (has_right, right), (design > 0, (space, parent))]
    partners += [(on, (space, child)) for on, child in children]
    expected = jnp.int32(0)
    for on, where in partners:
        expected = expected + on.astype(jnp.int32)

        @pl.when(on)
        def _(where=where):
            pl.semaphore_signal(barrier, inc=1, device_id=where, device_id_type=MESH)

    pl.semaphore_wait(barrier, expected)

    def u_copies(step, k):
        src, first = (u_ref, 0) if step == 0 else (level.at[step, 0], rows)
        low, high = k, rows - 1 - k
        return (
            remote(
                src.at[:, pl.ds(first + low, 1)], level.at[step, 0, :, pl.ds(2 * rows + low, 1)],
                u_send.at[step, 0, k], u_recv.at[step, 1, k], left,
            ),
            remote(
                src.at[:, pl.ds(first + high, 1)], level.at[step, 0, :, pl.ds(high, 1)],
                u_send.at[step, 1, k], u_recv.at[step, 0, k], right,
            ),
        )

    kind_copies = (
        remote(kind_ref, kind_right, side_send.at[0], side_recv.at[1], left),
        remote(kind_ref, kind_left, side_send.at[1], side_recv.at[0], right),
    )
    def source_copies(k):
        low, high = k, rows - 1 - k
        return (
            remote(
                source_ref.at[:, pl.ds(low, 1)], target.at[:, pl.ds(2 * rows + low, 1)],
                side_send.at[2 + 2 * k], side_recv.at[3 + 2 * k], left,
            ),
            remote(
                source_ref.at[:, pl.ds(high, 1)], target.at[:, pl.ds(high, 1)],
                side_send.at[3 + 2 * k], side_recv.at[2 + 2 * k], right,
            ),
        )

    def needed(last):
        return pl.ds(0, 1 if last else 2)

    def coef_side_copies(step, k, last):
        low, high = k, rows - 1 - k
        kept = needed(last)
        return (
            remote(
                coef.at[step, kept, pl.ds(rows + low, 1)], coef.at[step, kept, pl.ds(2 * rows + low, 1)],
                coef_side.at[step, 0, k], coef_recv.at[step, 2 * rows + low], left,
            ),
            remote(
                coef.at[step, kept, pl.ds(rows + high, 1)], coef.at[step, kept, pl.ds(high, 1)],
                coef_side.at[step, 1, k], coef_recv.at[step, high], right,
            ),
        )

    def tree_copy(step, child, row, last=False):
        where = coef.at[step, needed(last), pl.ds(row, 1)]
        return remote(
            where, where, coef_send.at[step, child, row], coef_recv.at[step, row], (space, children[child][1])
        )

    sides = (has_left, has_right)

    def on_sides(copies, action, also=None):
        for on, copy in zip(sides, copies):

            @pl.when(on if also is None else on & also)
            def _(copy=copy):
                action(copy)

    def recv_sides(copies, also=None):
        for on, copy in zip(sides, copies[::-1]):

            @pl.when(on if also is None else on & also)
            def _(copy=copy):
                copy.wait_recv()

    def start(copy):
        copy.start()

    def wait_send(copy):
        copy.wait_send()

    def forward(step, row, action, last=False):
        for child, (on, _) in enumerate(children):

            @pl.when(on)
            def _(child=child):
                action(tree_copy(step, child, row, last))

    def each_row(body):
        def one(k, carry):
            body(k)
            return carry

        lax.fori_loop(0, rows, one, 0)

    def but_last(body):
        def one(k, carry):
            body(k, False)
            return carry

        lax.fori_loop(0, rows - 1, one, 0)
        body(rows - 1, True)

    def side_rows(body):
        def both(k, last):
            @pl.when(has_left)
            def _():
                body(rows - 1 - k, last)

            @pl.when(has_right)
            def _():
                body(2 * rows + k, last)

        but_last(both)

    def leave(step):
        primal_coefficients(step)

        @pl.when(primal)
        def _():
            but_last(lambda k, last: on_sides(coef_side_copies(step, k, last), start))
            each_row(lambda k: forward(step, rows + k, start))

        each_row(lambda k: on_sides(u_copies(step, k), start))

    root = relay & (pair == 0)

    def take(step, row, last=False):
        tree_copy(step, 0, row, last).wait_recv()
        forward(step, row, start, last)

    def relay_coefficients(step):
        @pl.when(design > 0)
        def _():
            each_row(lambda k: take(step, rows + k))

        @pl.when(root)
        def _():
            side_rows(lambda row, last: take(step, row, last))

    def late_coefficients(step, k):
        @pl.when(has_left & (design > 0) & ~root)
        def _():
            take(step, rows - 1 - k, k == rows - 1)

        @pl.when(has_right & (design > 0) & ~root)
        def _():
            take(step, 2 * rows + k, k == rows - 1)

    def primal_coefficients(step):
        @pl.when(primal)
        def _():
            def row(r, carry):
                if step == 0:
                    p0, p1, p4 = u_ref[0, r], u_ref[1, r], u_ref[4, r]
                else:
                    p0, p1, p4 = (level[step, 0, f, rows + r] for f in (0, 1, 4))
                coef[step, 0, rows + r] = jnp.exp(0.5 * jnp.tanh(p4 - 0.5 * p0)) - 1.0
                coef[step, 1, rows + r] = jnp.tanh(p1)
                return carry

            lax.fori_loop(0, rows, row, 0)

    def blank(step):
        @pl.when(space == 0)
        def _():
            level[step, 0, :, lower] = jnp.zeros((FIELDS, rows, width_y, width_z), jnp.float32)
            coef[step, :, lower] = jnp.zeros((2, rows, width_y, width_z), jnp.float32)

        @pl.when(space == slabs - 1)
        def _():
            level[step, 0, :, upper] = jnp.zeros((FIELDS, rows, width_y, width_z), jnp.float32)
            coef[step, :, upper] = jnp.zeros((2, rows, width_y, width_z), jnp.float32)

    row_y = lax.broadcasted_iota(jnp.int32, (width_y, width_z), 0)
    row_z = lax.broadcasted_iota(jnp.int32, (width_y, width_z), 1)
    first_y, last_y = row_y == 0, row_y == width_y - 1
    first_z, last_z = row_z == 0, row_z == width_z - 1

    def shifts(plane):
        return (
            pltpu.roll(plane, 1, 0),
            pltpu.roll(plane, width_y - 1, 0),
            pltpu.roll(plane, 1, 1),
            pltpu.roll(plane, width_z - 1, 1),
        )

    edges = (first_y, last_y, first_z, last_z)

    def weight_row(step, r):
        centre = 1.0 + coef[step, 0, r]
        below = 0.5 * (centre + 1.0 + coef[step, 0, r - 1])
        above = 0.5 * (centre + 1.0 + coef[step, 0, r + 1])
        upwind = 1.0 + coef[step, 1, r]
        diagonal = damping[r] + upwind + below + above
        grid_row = space * rows + r - rows
        weight[0, r] = jnp.where(grid_row == 0, 0.0, below + upwind)
        weight[1, r] = jnp.where(grid_row == slabs * rows - 1, 0.0, above)
        for k, (near, edge) in enumerate(zip(shifts(centre), edges)):
            face = 0.5 * (centre + jnp.where(edge, 1.0, near))
            diagonal = diagonal + face
            weight[2 + k, r] = jnp.where(edge, 0.0, face)
        weight[6, r] = 1.0 / diagonal

    def weights(step, k):
        if k == 0:
            each_row(lambda i: weight_row(step, rows + i))
        else:

            def one(side, carry):
                weight_row(step, rows - k + side * (rows - 1 + 2 * k))
                return carry

            lax.fori_loop(0, 2, one, 0)

    def relax_row(src, dst, r, shift):
        planes = [src[f, r] for f in range(FIELDS)]
        for f in range(FIELDS):
            total = target[f, r] + weight[0, r] * src[f, r - 1] + weight[1, r] * src[f, r + 1]
            for k, near in enumerate(shifts(planes[f])):
                total = total + weight[2 + k, r] * near
            for h in range(FIELDS):
                total = total - coupling_ref[f, h] * planes[h]
            dst[f, r - shift] = total * weight[6, r]

    def sweep_own(step, stage):
        src, shift = level.at[step, stage - 1], 0
        if stage < SWEEPS:
            dst = level.at[step, stage]
        elif step < PSTEPS - 1:
            dst = level.at[step + 1, 0]
        else:
            dst, shift = out_ref, rows

        each_row(lambda k: relax_row(src, dst, rows + k, shift))

    def sweep_halo(step, k):
        def one(i, carry):
            stage, side = 1 + i // 2, i % 2
            out = k + 1 - stage
            r = rows - out + side * (rows - 1 + 2 * out)
            relax_row(level.at[step, stage - 1], level.at[step, stage], r, 0)
            return carry

        lax.fori_loop(0, 2 * k, one, 0)

    def spread_kinds(kinds, first):
        pick_b = lax.broadcasted_iota(jnp.int32, (width_z // ZB, width_z), 0)
        pick_z = lax.broadcasted_iota(jnp.int32, (width_z // ZB, width_z), 1)
        inside = (pick_z >= pick_b * ZB) & (pick_z < pick_b * ZB + ZB)
        for r in range(rows):
            cells = lax.dot_general(
                kinds[r].astype(jnp.float32), inside.astype(jnp.float32), (((0,), (0,)), ((), ())),
                preferred_element_type=jnp.float32,
            )
            damping[first + r] = 0.8 + jnp.where(cells == 1.0, 2.2, 0.0) + jnp.where(cells == 2.0, 0.7, 0.0)

    on_sides(kind_copies, start)
    leave(0)
    for k in range(SWEEPS - 1):
        on_sides(source_copies(k), start, primal)

    blank(0)
    level[0, 0, :, own] = u_ref[...]

    @pl.when(primal)
    def _():
        target[:, own] = source_ref[...]

        @pl.when(space == 0)
        def _():
            target[:, lower] = jnp.zeros((FIELDS, rows, width_y, width_z), jnp.float32)

        @pl.when(space == slabs - 1)
        def _():
            target[:, upper] = jnp.zeros((FIELDS, rows, width_y, width_z), jnp.float32)

    @pl.when(design > 0)
    def _():
        tangents, count = points_ref.shape
        mine = lax.broadcasted_iota(jnp.int32, (tangents, count), 0) == design - 1
        points = jnp.sum(jnp.where(mine, points_ref[...], 0), axis=0, keepdims=True)
        shapes = jnp.concatenate(
            [
                jnp.sum(jnp.where(mine, shapes_ref[f], 0.0), axis=0, keepdims=True)
                for f in range(FIELDS)
            ],
            axis=0,
        )

        def row(r, carry):
            cell = (space * rows + r - rows) * width_z + lax.broadcasted_iota(
                jnp.int32, (width_z, count), 0
            )
            hit = (points == cell).astype(jnp.float32)
            wall = lax.dot_general(
                shapes, hit, (((1,), (1,)), ((), ())),
                precision=lax.Precision.HIGHEST, preferred_element_type=jnp.float32,
            )
            for f in range(FIELDS):
                line = jnp.broadcast_to(wall[f : f + 1], (width_y, width_z))
                target[f, r] = jnp.where(first_y, line, 0.0)
            return carry

        lax.fori_loop(0, wide, row, 0)

    spread_kinds(kind_ref, rows)

    for step in range(PSTEPS):
        if step > 0:
            leave(step)
            blank(step)

        relay_coefficients(step)

        if step == 0:
            recv_sides(kind_copies)

            @pl.when(has_left)
            def _():
                spread_kinds(kind_left, 0)

            @pl.when(has_right)
            def _():
                spread_kinds(kind_right, 2 * rows)

            @pl.when(space == 0)
            def _():
                damping[lower] = jnp.zeros((rows, width_y, width_z), jnp.float32)

            @pl.when(space == slabs - 1)
            def _():
                damping[upper] = jnp.zeros((rows, width_y, width_z), jnp.float32)

        for k in range(SWEEPS):
            late_coefficients(step, k)
            weights(step, k)
            recv_sides(u_copies(step, k))
            if k > 0:
                if step == 0:
                    recv_sides(source_copies(k - 1), primal)
                sweep_halo(step, k)
            sweep_own(step, k + 1)

    on_sides(kind_copies, wait_send)
    for k in range(SWEEPS - 1):
        on_sides(source_copies(k), wait_send, primal)
    for step in range(PSTEPS):
        each_row(lambda k: on_sides(u_copies(step, k), wait_send))

        @pl.when(primal)
        def _():
            but_last(lambda k, last: on_sides(coef_side_copies(step, k, last), wait_send))

        each_row(lambda k: forward(step, rows + k, wait_send))
        side_rows(lambda row, last: forward(step, row, wait_send, last))


def shards(states, source, cell_kind, wall_points, point_shape, coupling):
    member_state = states[0]
    fields, rows, width_y, width_z = member_state.shape
    slabs = lax.axis_size("space")
    kinds = jnp.transpose(cell_kind, (0, 2, 1))
    shapes = jnp.transpose(point_shape, (2, 0, 1))
    vmem = pl.BlockSpec(memory_space=pltpu.VMEM)
    wide = 3 * rows
    out = pl.pallas_call(
        functools.partial(kernel, slabs, rows),
        name="sweeps",
        out_shape=pltpu.VMEM(member_state.shape, jnp.float32),
        in_specs=[vmem] * 5 + [pl.BlockSpec(memory_space=pltpu.SMEM)],
        out_specs=vmem,
        scratch_shapes=[
            pltpu.VMEM((PSTEPS, SWEEPS, fields, wide, width_y, width_z), jnp.float32),
            pltpu.VMEM((PSTEPS, 2, wide, width_y, width_z), jnp.float32),
            pltpu.VMEM((7, wide, width_y, width_z), jnp.float32),
            pltpu.VMEM((fields, wide, width_y, width_z), jnp.float32),
            pltpu.VMEM((wide, width_y, width_z), jnp.float32),
            pltpu.VMEM(kinds.shape, jnp.int32),
            pltpu.VMEM(kinds.shape, jnp.int32),
            pltpu.SemaphoreType.DMA((PSTEPS, 2, rows)),
            pltpu.SemaphoreType.DMA((PSTEPS, 2, rows)),
            pltpu.SemaphoreType.DMA((2 * rows,)),
            pltpu.SemaphoreType.DMA((2 * rows,)),
            pltpu.SemaphoreType.DMA((PSTEPS, 2, rows)),
            pltpu.SemaphoreType.DMA((PSTEPS, 4, wide)),
            pltpu.SemaphoreType.DMA((PSTEPS, wide)),
        ],
        compiler_params=pltpu.CompilerParams(collective_id=0, has_side_effects=True),
    )(member_state, source, kinds, wall_points, shapes, coupling)
    return out[None]


def solution(mesh):
    in_specs = (
        P("design", None, "space", None, None),
        P(None, "space", None, None),
        P("space", None, None),
        P(),
        P(),
        P(),
    )
    out_specs = P("design", None, "space", None, None)
    return jax.shard_map(shards, mesh=mesh, in_specs=in_specs, out_specs=out_specs, check_vma=False)
```

```python
import functools

import jax
import jax.numpy as jnp
from jax import lax
from jax.experimental import pallas as pl
from jax.experimental.pallas import tpu as pltpu
from jax.sharding import PartitionSpec as P

ZB = 8
SWEEPS = 4
PSTEPS = 2
FIELDS = 5
MESH = pl.DeviceIdType.MESH


def kernel(
    slabs, rows,
    u_ref, source_ref, kind_ref, points_ref, shapes_ref, coupling_ref,
    out_ref,
    level, coef, weight, target, damping, kind_left, kind_right,
    u_send, u_recv, side_send, side_recv, coef_side, coef_send, coef_recv,
):
    space = lax.axis_index("space")
    design = lax.axis_index("design")
    width_y, width_z = u_ref.shape[2], u_ref.shape[3]
    wide = 3 * rows
    own = slice(rows, 2 * rows)
    lower = slice(0, rows)
    upper = slice(2 * rows, wide)

    core = design % 2
    ring = (design // 2) % 4
    pair = design // 8
    primal = design == 0
    has_left = space > 0
    has_right = space < slabs - 1
    relay = core == 0
    to_partner = relay
    to_pair = relay & (pair == 0)
    to_next = relay & (pair == 0) & (ring < 2)
    children = (
        (to_next, design + 2),
        (primal, design + 6),
        (to_pair, design + 8),
        (to_partner, design + 1),
    )
    last = ring // 3
    parent = core * (design - 1) + (1 - core) * (
        pair * (design - 8) + (1 - pair) * (1 - last) * (design - 2)
    )

    def remote(src, dst, send, recv, where):
        return pltpu.make_async_remote_copy(
            src_ref=src, dst_ref=dst, send_sem=send, recv_sem=recv, device_id=where, device_id_type=MESH
        )

    left = (space - 1, design)
    right = (space + 1, design)

    barrier = pltpu.get_barrier_semaphore()
    partners = [(has_left, left), (has_right, right), (design > 0, (space, parent))]
    partners += [(on, (space, child)) for on, child in children]
    expected = jnp.int32(0)
    for on, where in partners:
        expected = expected + on.astype(jnp.int32)

        @pl.when(on)
        def _(where=where):
            pl.semaphore_signal(barrier, inc=1, device_id=where, device_id_type=MESH)

    pl.semaphore_wait(barrier, expected)

    def u_copies(step, k):
        src, first = (u_ref, 0) if step == 0 else (level.at[step, 0], rows)
        low, high = k, rows - 1 - k
        return (
            remote(
                src.at[:, pl.ds(first + low, 1)], level.at[step, 0, :, pl.ds(2 * rows + low, 1)],
                u_send.at[step, 0, k], u_recv.at[step, 1, k], left,
            ),
            remote(
                src.at[:, pl.ds(first + high, 1)], level.at[step, 0, :, pl.ds(high, 1)],
                u_send.at[step, 1, k], u_recv.at[step, 0, k], right,
            ),
        )

    kind_copies = (
        remote(kind_ref, kind_right, side_send.at[0], side_recv.at[1], left),
        remote(kind_ref, kind_left, side_send.at[1], side_recv.at[0], right),
    )
    def source_copies(k):
        low, high = k, rows - 1 - k
        return (
            remote(
                source_ref.at[:, pl.ds(low, 1)], target.at[:, pl.ds(2 * rows + low, 1)],
                side_send.at[2 + 2 * k], side_recv.at[3 + 2 * k], left,
            ),
            remote(
                source_ref.at[:, pl.ds(high, 1)], target.at[:, pl.ds(high, 1)],
                side_send.at[3 + 2 * k], side_recv.at[2 + 2 * k], right,
            ),
        )

    def coef_side_copies(step, k):
        low, high = k, rows - 1 - k
        return (
            remote(
                coef.at[step, :, pl.ds(rows + low, 1)], coef.at[step, :, pl.ds(2 * rows + low, 1)],
                coef_side.at[step, 0, k], coef_recv.at[step, 2 * rows + low], left,
            ),
            remote(
                coef.at[step, :, pl.ds(rows + high, 1)], coef.at[step, :, pl.ds(high, 1)],
                coef_side.at[step, 1, k], coef_recv.at[step, high], right,
            ),
        )

    def tree_copy(step, child, row):
        where = coef.at[step, :, pl.ds(row, 1)]
        return remote(
            where, where, coef_send.at[step, child, row], coef_recv.at[step, row], (space, children[child][1])
        )

    sides = (has_left, has_right)

    def on_sides(copies, action, also=None):
        for on, copy in zip(sides, copies):

            @pl.when(on if also is None else on & also)
            def _(copy=copy):
                action(copy)

    def recv_sides(copies, also=None):
        for on, copy in zip(sides, copies[::-1]):

            @pl.when(on if also is None else on & also)
            def _(copy=copy):
                copy.wait_recv()

    def start(copy):
        copy.start()

    def wait_send(copy):
        copy.wait_send()

    def forward(step, row, action):
        for child, (on, _) in enumerate(children):

            @pl.when(on)
            def _(child=child):
                action(tree_copy(step, child, row))

    def each_row(body):
        def one(k, carry):
            body(k)
            return carry

        lax.fori_loop(0, rows, one, 0)

    def side_rows(body):
        def both(k):
            @pl.when(has_left)
            def _():
                body(rows - 1 - k)

            @pl.when(has_right)
            def _():
                body(2 * rows + k)

        each_row(both)

    def leave(step):
        primal_coefficients(step)

        @pl.when(primal)
        def _():
            each_row(lambda k: on_sides(coef_side_copies(step, k), start))
            each_row(lambda k: forward(step, rows + k, start))

        if step > 0:
            each_row(lambda k: on_sides(u_copies(step, k), start))
        else:
            for k in range(rows):
                on_sides(u_copies(0, k), start)
                if k > 0:
                    on_sides(source_copies(k - 1), start, primal)

    root = relay & (pair == 0)

    def take(step, row):
        tree_copy(step, 0, row).wait_recv()
        forward(step, row, start)

    def relay_coefficients(step):
        @pl.when(design > 0)
        def _():
            each_row(lambda k: take(step, rows + k))

        @pl.when(root)
        def _():
            side_rows(lambda row: take(step, row))

    def late_coefficients(step, k):
        @pl.when(has_left & (design > 0) & ~root)
        def _():
            take(step, rows - 1 - k)

        @pl.when(has_right & (design > 0) & ~root)
        def _():
            take(step, 2 * rows + k)

    def primal_coefficients(step):
        @pl.when(primal)
        def _():
            def row(r, carry):
                if step == 0:
                    p0, p1, p4 = u_ref[0, r], u_ref[1, r], u_ref[4, r]
                else:
                    p0, p1, p4 = (level[step, 0, f, rows + r] for f in (0, 1, 4))
                coef[step, 0, rows + r] = jnp.exp(0.5 * jnp.tanh(p4 - 0.5 * p0)) - 1.0
                coef[step, 1, rows + r] = jnp.tanh(p1)
                return carry

            lax.fori_loop(0, rows, row, 0)

    def blank(step):
        @pl.when(space == 0)
        def _():
            level[step, 0, :, lower] = jnp.zeros((FIELDS, rows, width_y, width_z), jnp.float32)
            coef[step, :, lower] = jnp.zeros((2, rows, width_y, width_z), jnp.float32)

        @pl.when(space == slabs - 1)
        def _():
            level[step, 0, :, upper] = jnp.zeros((FIELDS, rows, width_y, width_z), jnp.float32)
            coef[step, :, upper] = jnp.zeros((2, rows, width_y, width_z), jnp.float32)

    row_y = lax.broadcasted_iota(jnp.int32, (width_y, width_z), 0)
    row_z = lax.broadcasted_iota(jnp.int32, (width_y, width_z), 1)
    first_y, last_y = row_y == 0, row_y == width_y - 1
    first_z, last_z = row_z == 0, row_z == width_z - 1

    def shifts(plane):
        return (
            pltpu.roll(plane, 1, 0),
            pltpu.roll(plane, width_y - 1, 0),
            pltpu.roll(plane, 1, 1),
            pltpu.roll(plane, width_z - 1, 1),
        )

    edges = (first_y, last_y, first_z, last_z)

    def weight_row(step, r):
        centre = 1.0 + coef[step, 0, r]
        below = 0.5 * (centre + 1.0 + coef[step, 0, r - 1])
        above = 0.5 * (centre + 1.0 + coef[step, 0, r + 1])
        upwind = 1.0 + coef[step, 1, r]
        diagonal = damping[r] + upwind + below + above
        grid_row = space * rows + r - rows
        weight[0, r] = jnp.where(grid_row == 0, 0.0, below + upwind)
        weight[1, r] = jnp.where(grid_row == slabs * rows - 1, 0.0, above)
        for k, (near, edge) in enumerate(zip(shifts(centre), edges)):
            face = 0.5 * (centre + jnp.where(edge, 1.0, near))
            diagonal = diagonal + face
            weight[2 + k, r] = jnp.where(edge, 0.0, face)
        weight[6, r] = 1.0 / diagonal

    def weights(step, k):
        if k == 0:
            each_row(lambda i: weight_row(step, rows + i))
        else:

            def one(side, carry):
                weight_row(step, rows - k + side * (rows - 1 + 2 * k))
                return carry

            lax.fori_loop(0, 2, one, 0)

    def relax_row(src, dst, r, shift):
        planes = [src[f, r] for f in range(FIELDS)]
        for f in range(FIELDS):
            total = target[f, r] + weight[0, r] * src[f, r - 1] + weight[1, r] * src[f, r + 1]
            for k, near in enumerate(shifts(planes[f])):
                total = total + weight[2 + k, r] * near
            for h in range(FIELDS):
                total = total - coupling_ref[f, h] * planes[h]
            dst[f, r - shift] = total * weight[6, r]

    def sweep_own(step, stage):
        src, shift = level.at[step, stage - 1], 0
        if stage < SWEEPS:
            dst = level.at[step, stage]
        elif step < PSTEPS - 1:
            dst = level.at[step + 1, 0]
        else:
            dst, shift = out_ref, rows

        each_row(lambda k: relax_row(src, dst, rows + k, shift))

    def sweep_halo(step, k):
        def one(i, carry):
            stage, side = 1 + i // 2, i % 2
            out = k + 1 - stage
            r = rows - out + side * (rows - 1 + 2 * out)
            relax_row(level.at[step, stage - 1], level.at[step, stage], r, 0)
            return carry

        lax.fori_loop(0, 2 * k, one, 0)

    def spread_kinds(kinds, first):
        pick_b = lax.broadcasted_iota(jnp.int32, (width_z // ZB, width_z), 0)
        pick_z = lax.broadcasted_iota(jnp.int32, (width_z // ZB, width_z), 1)
        inside = (pick_z >= pick_b * ZB) & (pick_z < pick_b * ZB + ZB)
        for r in range(rows):
            cells = lax.dot_general(
                kinds[r].astype(jnp.float32), inside.astype(jnp.float32), (((0,), (0,)), ((), ())),
                preferred_element_type=jnp.float32,
            )
            damping[first + r] = 0.8 + jnp.where(cells == 1.0, 2.2, 0.0) + jnp.where(cells == 2.0, 0.7, 0.0)

    on_sides(kind_copies, start)
    leave(0)

    blank(0)
    level[0, 0, :, own] = u_ref[...]

    @pl.when(primal)
    def _():
        target[:, own] = source_ref[...]

        @pl.when(space == 0)
        def _():
            target[:, lower] = jnp.zeros((FIELDS, rows, width_y, width_z), jnp.float32)

        @pl.when(space == slabs - 1)
        def _():
            target[:, upper] = jnp.zeros((FIELDS, rows, width_y, width_z), jnp.float32)

    @pl.when(design > 0)
    def _():
        tangents, count = points_ref.shape
        mine = lax.broadcasted_iota(jnp.int32, (tangents, count), 0) == design - 1
        points = jnp.sum(jnp.where(mine, points_ref[...], 0), axis=0, keepdims=True)
        shapes = jnp.concatenate(
            [
                jnp.sum(jnp.where(mine, shapes_ref[f], 0.0), axis=0, keepdims=True)
                for f in range(FIELDS)
            ],
            axis=0,
        )

        def row(r, carry):
            cell = (space * rows + r - rows) * width_z + lax.broadcasted_iota(
                jnp.int32, (width_z, count), 0
            )
            hit = (points == cell).astype(jnp.float32)
            wall = lax.dot_general(
                shapes, hit, (((1,), (1,)), ((), ())),
                precision=lax.Precision.HIGHEST, preferred_element_type=jnp.float32,
            )
            for f in range(FIELDS):
                line = jnp.broadcast_to(wall[f : f + 1], (width_y, width_z))
                target[f, r] = jnp.where(first_y, line, 0.0)
            return carry

        lax.fori_loop(0, wide, row, 0)

    spread_kinds(kind_ref, rows)

    for step in range(PSTEPS):
        if step > 0:
            leave(step)
            blank(step)

        relay_coefficients(step)

        if step == 0:
            recv_sides(kind_copies)

            @pl.when(has_left)
            def _():
                spread_kinds(kind_left, 0)

            @pl.when(has_right)
            def _():
                spread_kinds(kind_right, 2 * rows)

            @pl.when(space == 0)
            def _():
                damping[lower] = jnp.zeros((rows, width_y, width_z), jnp.float32)

            @pl.when(space == slabs - 1)
            def _():
                damping[upper] = jnp.zeros((rows, width_y, width_z), jnp.float32)

        for k in range(SWEEPS):
            late_coefficients(step, k)
            weights(step, k)
            recv_sides(u_copies(step, k))
            if k > 0:
                if step == 0:
                    recv_sides(source_copies(k - 1), primal)
                sweep_halo(step, k)
            sweep_own(step, k + 1)

    on_sides(kind_copies, wait_send)
    for k in range(SWEEPS - 1):
        on_sides(source_copies(k), wait_send, primal)
    for step in range(PSTEPS):
        each_row(lambda k: on_sides(u_copies(step, k), wait_send))

        @pl.when(primal)
        def _():
            each_row(lambda k: on_sides(coef_side_copies(step, k), wait_send))

        each_row(lambda k: forward(step, rows + k, wait_send))
        side_rows(lambda row: forward(step, row, wait_send))


def shards(states, source, cell_kind, wall_points, point_shape, coupling):
    member_state = states[0]
    fields, rows, width_y, width_z = member_state.shape
    slabs = lax.axis_size("space")
    kinds = jnp.transpose(cell_kind, (0, 2, 1))
    shapes = jnp.transpose(point_shape, (2, 0, 1))
    vmem = pl.BlockSpec(memory_space=pltpu.VMEM)
    wide = 3 * rows
    out = pl.pallas_call(
        functools.partial(kernel, slabs, rows),
        name="sweeps",
        out_shape=pltpu.VMEM(member_state.shape, jnp.float32),
        in_specs=[vmem] * 5 + [pl.BlockSpec(memory_space=pltpu.SMEM)],
        out_specs=vmem,
        scratch_shapes=[
            pltpu.VMEM((PSTEPS, SWEEPS, fields, wide, width_y, width_z), jnp.float32),
            pltpu.VMEM((PSTEPS, 2, wide, width_y, width_z), jnp.float32),
            pltpu.VMEM((7, wide, width_y, width_z), jnp.float32),
            pltpu.VMEM((fields, wide, width_y, width_z), jnp.float32),
            pltpu.VMEM((wide, width_y, width_z), jnp.float32),
            pltpu.VMEM(kinds.shape, jnp.int32),
            pltpu.VMEM(kinds.shape, jnp.int32),
            pltpu.SemaphoreType.DMA((PSTEPS, 2, rows)),
            pltpu.SemaphoreType.DMA((PSTEPS, 2, rows)),
            pltpu.SemaphoreType.DMA((2 * rows,)),
            pltpu.SemaphoreType.DMA((2 * rows,)),
            pltpu.SemaphoreType.DMA((PSTEPS, 2, rows)),
            pltpu.SemaphoreType.DMA((PSTEPS, 4, wide)),
            pltpu.SemaphoreType.DMA((PSTEPS, wide)),
        ],
        compiler_params=pltpu.CompilerParams(collective_id=0, has_side_effects=True),
    )(member_state, source, kinds, wall_points, shapes, coupling)
    return out[None]


def solution(mesh):
    in_specs = (
        P("design", None, "space", None, None),
        P(None, "space", None, None),
        P("space", None, None),
        P(),
        P(),
        P(),
    )
    out_specs = P("design", None, "space", None, None)
    return jax.shard_map(shards, mesh=mesh, in_specs=in_specs, out_specs=out_specs, check_vma=False)
```
